32 devices in a mesh: table: 16 (over z, y, x), ctx: 2 (over core).
Axes of the slice: x: 2, y: 2, z: 4, core: 2. Of those that a mesh axis runs over, the one named last changes fastest.
Arguments:
- item_table: float32 [32768, 256], P('table'), may hold values from -3 to 3
- serve_rows: int32 [256, 512], P('table', 'ctx'), may hold values from 0 to 2047, as said below
- token_slots: int32 [16, 2048, 4], P('table', 'ctx'), may hold values from 0 to 4095
- lengths: int32 [16], P('table'), may hold values from 1 to 2048, as said below
- w_proj: bfloat16 [256, 2048], replicated, may hold values from -0.375 to 0.375
- w_out: bfloat16 [512, 256], replicated, may hold values from -0.25 to 0.25
- grad_out: bfloat16 [16, 2048, 256], P('table', 'ctx'), may hold values from -6 to 6
Outputs:
- layer_out: bfloat16 [16, 2048, 256], P('table', 'ctx')
- grad_table: float32 [32768, 256], P(('table', 'ctx'))
The draws below stay inside these ranges and needn't reach their ends.
Inputs may be any that keep to these rules, and one draw needn't show every extreme that they name: `serve_rows`: the 256 rows that one owner serves to one requesting device are distinct. `lengths`: some history has all 2048 actions.
All inputs are finite; a program needn't handle non-finite values.
Results may differ from the reference program's by a relative error of at most 0.009.
Values may be sent and summed in bfloat16 or wider, within the bound.
No kernel may reach another device: no remote copies, remote signals or barrier semaphores. Data moves between devices by JAX's collectives and lax.ppermute only.
A program may use at most 192 MiB of HBM per device.

```python
import math
import jax
import jax.numpy as jnp
import numpy as np
from jax import lax

D = 256
HEADS = 4
HEAD = 128
FEATS = 4
TOK_DEV = 1024
ROWS_DEV = 2048
HD = 512
LEN = 2048
BATCH = 16
CAP = 256
SLOTS = 4096
SERVE = 256
SERVE_COLS = 512
TABLE_ROWS = 32768


def draw_serve_rows(key, part):
    scores = jax.random.randint(key, (SERVE, SERVE_COLS // CAP, ROWS_DEV), 0, 2 ** 30)
    order = jnp.argsort(scores, axis=-1, stable=True)
    return order[..., :CAP].reshape(SERVE, SERVE_COLS).astype(jnp.int32)


def draw_lengths(key, part):
    first_key = jax.random.fold_in(key, 11)
    second_key = jax.random.fold_in(key, 23)
    drawn = jax.random.randint(first_key, (BATCH,), 1, LEN + 1)
    longest = jax.random.randint(second_key, (), 0, BATCH)
    return jnp.where(jnp.arange(BATCH) == longest, LEN, drawn).astype(jnp.int32)


def with_ends(entries, own_key, least, high):
    index_at = [jax.random.randint(jax.random.fold_in(own_key, axis), (), 0, length) for axis, length in enumerate(entries.shape)]
    main_axis = entries.shape.index(max(entries.shape))
    next_to = index_at[:main_axis] + [(index_at[main_axis] + 1) % entries.shape[main_axis]] + index_at[main_axis + 1:]
    return entries.at[tuple(index_at)].set(least).at[tuple(next_to)].set(high)


def block_levels(key, shape, shards, smallest, largest):
    level, own = 1.0, jax.random.fold_in(key, 6)
    for axis_at, parts in shards:
        steps = jnp.exp(jax.random.uniform(jax.random.fold_in(own, axis_at), (parts,), jnp.float32, smallest / len(shards), largest / len(shards)))
        level = level * jnp.repeat(steps, shape[axis_at] // parts).reshape([-1 if axis == axis_at else 1 for axis in range(len(shape))])
    return level


def cumulative_ranks(number_of, lean):
    loads = [(1 << 20) // math.isqrt(grade ** lean) + 1 for grade in range(1, number_of + 1)]
    spread = 1 + sum(loads) // (1 << 30)
    return np.cumsum(np.array([max(1, weight // spread) for weight in loads]))


def ranked_ids(own_key, shape, count, skew):
    listing = cumulative_ranks(count, skew)
    lot = jax.random.randint(jax.random.fold_in(own_key, 1), shape, 0, int(listing[count - 1]))
    grade = jnp.searchsorted(jnp.asarray(listing, jnp.int32), lot, side="right")
    return jax.random.permutation(jax.random.fold_in(own_key, 2), count)[grade].astype(jnp.int32)


def normal_values(own_key, dims, width, limit, shards=(), held_as=jnp.bfloat16):
    result = jax.random.normal(own_key, dims, jnp.float32) * width
    if len(shards) > 0:
        result = block_levels(own_key, dims, shards, -0.22, 0.18) * result
    return jnp.clip(result, min=-limit, max=limit).astype(held_as)


def setup_inputs(seed: int = 0) -> dict:
    key_of = jax.random.split(jax.random.key(seed), 8)
    item_table = normal_values(key_of[0], (TABLE_ROWS, D), 0.5, 3.0, ((0, 16),), jnp.float32)
    serve_rows = draw_serve_rows(jax.random.fold_in(key_of[7], 71), 0)
    token_slots = with_ends(ranked_ids(key_of[2], (BATCH, LEN, FEATS), SLOTS, 1), jax.random.fold_in(key_of[2], 3), 0, SLOTS - 1).astype(jnp.int32)
    lengths = draw_lengths(jax.random.fold_in(key_of[7], 71), 0)
    w_proj = normal_values(key_of[4], (D, 4 * HD), D ** -0.5, 0.375)
    w_out = normal_values(key_of[5], (HD, D), HD ** -0.5, 0.25)
    grad_out = normal_values(key_of[6], (BATCH, LEN, D), 1.0, 6.0, ((0, 16), (1, 2)))
    return {"item_table": item_table, "serve_rows": serve_rows, "token_slots": token_slots, "lengths": lengths, "w_proj": w_proj, "w_out": w_out, "grad_out": grad_out}


epsilon = 1e-05

def silu_slope(inputs):
    sigmoid_value = jax.nn.sigmoid(inputs)
    return sigmoid_value * (1.0 + inputs * (1.0 - sigmoid_value))

def normalize(inputs):
    centred = inputs - lax.optimization_barrier(jnp.mean(inputs, axis=-1, keepdims=True))
    inverse = lax.rsqrt(lax.optimization_barrier(jnp.mean(centred * centred, axis=-1, keepdims=True)) + epsilon)
    return (centred * inverse, inverse)

def normalize_wide(inputs):
    middle = lax.optimization_barrier(jnp.mean(inputs, axis=-1, keepdims=True))
    square_mean = lax.optimization_barrier(jnp.mean(inputs * inputs, axis=-1, keepdims=True))
    inverse = lax.rsqrt(square_mean - middle * middle + epsilon)
    return ((inputs - middle) * inverse, inverse)

def norm_back(gradients, normed, inverse):
    return (gradients - lax.optimization_barrier(jnp.mean(gradients, axis=-1, keepdims=True)) - normed * lax.optimization_barrier(jnp.mean(gradients * normed, axis=-1, keepdims=True))) * inverse

def rounded(inputs):
    return lax.optimization_barrier(inputs.astype(jnp.bfloat16)).astype(jnp.float32)

def per_history(embedded, cotangent, length, w_proj, w_out):
    positions = jnp.arange(LEN, dtype=jnp.int32)
    valid_rows = positions < length
    normal_x, input_inverse = normalize(embedded)
    normed_input = normal_x.astype(jnp.bfloat16)
    pre_act = jnp.dot(normed_input, w_proj, preferred_element_type=jnp.float32)
    activated = jax.nn.silu(pre_act).astype(jnp.bfloat16)
    gating, values, queries, keyrows = jnp.split(activated, 4, axis=1)
    score_scale = HEAD ** (-0.5)
    heads_q = queries.astype(jnp.float32).reshape(LEN, HEADS, HEAD)
    heads_k = keyrows.astype(jnp.float32).reshape(LEN, HEADS, HEAD)
    heads_v = values.astype(jnp.float32).reshape(LEN, HEADS, HEAD)
    allowed = ((positions[None, :] <= positions[:, None]) & (positions[None, :] < length)).astype(jnp.float32)
    scaled = jnp.einsum('ihd,jhd->hij', heads_q, heads_k) * score_scale
    weights = rounded(jax.nn.silu(scaled) * allowed)
    attended = jnp.einsum('hij,jhd->ihd', weights, heads_v).reshape(LEN, HD)
    normed_out, out_inverse = normalize_wide(attended)
    gated_rows = (normed_out * gating.astype(jnp.float32)).astype(jnp.bfloat16)
    mixed_rows = jnp.dot(gated_rows, w_out, preferred_element_type=jnp.float32)
    layer_out = jnp.where(valid_rows[:, None], embedded + mixed_rows, 0.0).astype(jnp.bfloat16)
    masked_g = jnp.where(valid_rows[:, None], cotangent, jnp.zeros_like(cotangent))
    grad_gated = jnp.dot(masked_g, w_out.T, preferred_element_type=jnp.float32)
    grad_gating = grad_gated * normed_out
    grad_attended = rounded(norm_back(grad_gated * gating.astype(jnp.float32), normed_out, out_inverse))
    heads_g = grad_attended.reshape(LEN, HEADS, HEAD)
    grad_weights = jnp.einsum('ihd,jhd->hij', heads_g, heads_v)
    grad_scores = rounded(grad_weights * silu_slope(scaled) * score_scale * allowed)
    grad_q = jnp.einsum('hij,jhd->ihd', grad_scores, heads_k).reshape(LEN, HD)
    grad_k = jnp.einsum('hij,ihd->jhd', grad_scores, heads_q).reshape(LEN, HD)
    grad_v = jnp.einsum('hij,ihd->jhd', weights, heads_g).reshape(LEN, HD)
    grad_act = jnp.concatenate([grad_gating, grad_v, grad_q, grad_k], axis=1)
    grad_pre = (grad_act * silu_slope(pre_act)).astype(jnp.bfloat16)
    grad_x = jnp.dot(grad_pre, w_proj.T, preferred_element_type=jnp.float32)
    grad_emb = masked_g.astype(jnp.float32) + norm_back(grad_x, normal_x, input_inverse)
    return (layer_out, grad_emb)

def reference(item_table, serve_rows, token_slots, lengths, w_proj, w_out, grad_out):
    served_rows = serve_rows.reshape(BATCH, BATCH, LEN // TOK_DEV, CAP)
    owner_index = token_slots // CAP
    within = token_slots % CAP
    shard_index = (jnp.arange(LEN, dtype=jnp.int32) // TOK_DEV)[None, :, None]
    batch_index = jnp.arange(BATCH, dtype=jnp.int32)[:, None, None]
    row_ids = (owner_index * ROWS_DEV + served_rows[owner_index, batch_index, shard_index, within]).astype(jnp.int32)
    embedded = item_table[row_ids[..., 0]]
    for feature in range(1, FEATS):
        embedded = embedded + item_table[row_ids[..., feature]]

    def one_history(items):
        return per_history(items[0], items[1], items[2], w_proj, w_out)
    layer_out, grad_emb = lax.map(one_history, (embedded, grad_out, lengths))
    flat_grads = grad_emb.reshape(-1, D)
    grad_table = jnp.zeros((TABLE_ROWS, D), jnp.float32)
    for feature in range(FEATS):
        grad_table = grad_table + jax.ops.segment_sum(flat_grads, row_ids[..., feature].reshape(-1), num_segments=TABLE_ROWS)
    return (layer_out, grad_table)
```

```python
import functools

import jax
import jax.numpy as jnp
from jax import lax
from jax.experimental import pallas as pl
from jax.experimental.pallas import tpu as pltpu
from jax.sharding import PartitionSpec as P

HEAD = 128
epsilon = 1e-05
F32 = jnp.float32
BF16 = jnp.bfloat16
ROWS = 256
BLOCK = 512


def mm(lhs, rhs):
    return lax.dot_general(lhs, rhs, (((1,), (0,)), ((), ())), preferred_element_type=F32)


def mm_rt(lhs, rhs):
    return lax.dot_general(lhs, rhs, (((1,), (1,)), ((), ())), preferred_element_type=F32)


def mm_lt(lhs, rhs):
    return lax.dot_general(lhs, rhs, (((0,), (0,)), ((), ())), preferred_element_type=F32)


def rows_at(start, count):
    return pl.ds(pl.multiple_of(start, count), count)


def vmem():
    return pl.BlockSpec(memory_space=pltpu.VMEM)


def smem():
    return pl.BlockSpec(memory_space=pltpu.SMEM)


def call(body, out_shape, in_specs, scratch=(), flops=0, moved=0):
    return pl.pallas_call(
        body,
        out_shape=out_shape,
        in_specs=in_specs,
        out_specs=jax.tree.map(lambda _: vmem(), out_shape),
        scratch_shapes=list(scratch),
        compiler_params=pltpu.CompilerParams(vmem_limit_bytes=60 * 1024 * 1024),
        cost_estimate=pl.CostEstimate(flops=flops, bytes_accessed=moved, transcendentals=0),
    )


def column(row, count):
    return jnp.transpose(jnp.broadcast_to(row, (HEAD, count)))


def serve_body(ids_ref, table_ref, out_ref, table_low, hot):
    table_low[...] = table_ref[...].astype(BF16)
    table_rows = table_ref.shape[0]
    lanes = lax.broadcasted_iota(jnp.int32, (BLOCK, HEAD), 1)

    def step(at, carry):
        ids = column(ids_ref[pl.ds(at, 1), :], BLOCK)
        for part in range(table_rows // HEAD):
            hit = ids == lanes + part * HEAD
            hot[:, part * HEAD : (part + 1) * HEAD] = jnp.where(hit, 1.0, 0.0).astype(BF16)
        out_ref[rows_at(at * BLOCK, BLOCK), :] = mm(hot[...], table_low[...]).astype(BF16)
        return carry

    lax.fori_loop(0, ids_ref.shape[0], step, 0)


def embed_body(slots_ref, fetched_ref, embedded_ref, normed_ref, hot):
    slot_total = fetched_ref.shape[0]
    lanes = lax.broadcasted_iota(jnp.int32, (ROWS, HEAD), 1)

    def step(at, carry):
        ids = [
            column(slots_ref[feature : feature + 1, rows_at(at * ROWS, ROWS)], ROWS)
            for feature in range(slots_ref.shape[0])
        ]
        for part in range(slot_total // HEAD):
            here = lanes + part * HEAD
            count = jnp.where(ids[0] == here, 1.0, 0.0)
            for one in ids[1:]:
                count = count + jnp.where(one == here, 1.0, 0.0)
            hot[:, part * HEAD : (part + 1) * HEAD] = count.astype(BF16)
        value = mm(hot[...], fetched_ref[...])
        where = rows_at(at * ROWS, ROWS)
        embedded_ref[where, :] = value
        normed_ref[where, :] = normalize(value)[0].astype(BF16)
        return carry

    lax.fori_loop(0, embedded_ref.shape[0] // ROWS, step, 0)


def normalize(inputs):
    centred = inputs - jnp.mean(inputs, axis=-1, keepdims=True)
    inverse = lax.rsqrt(jnp.mean(centred * centred, axis=-1, keepdims=True) + epsilon)
    return (centred * inverse, inverse)


def silu_parts(inputs):
    half = inputs * 0.5
    above = 1.0 + jnp.tanh(half)
    value = half * above
    return value, above


def slope_of(inputs):
    value, above = silu_parts(inputs)
    return 0.5 * above * (1.0 + inputs - value)


def forward_body(
    place_ref, xm_ref, xo_ref, gm_ref, go_ref, w_ref, wout_ref,
    x_ref, g_ref, act_ref, att_ref, stats_ref,
):
    mine, length = place_ref[0], place_ref[1]
    count = xm_ref.shape[0]
    total = x_ref.shape[0]
    width = att_ref.shape[1]
    x_ref[rows_at(mine * count, count), :] = xm_ref[...]
    x_ref[rows_at((1 - mine) * count, count), :] = xo_ref[...]
    g_ref[rows_at(mine * count, count), :] = gm_ref[...]
    g_ref[rows_at((1 - mine) * count, count), :] = go_ref[...]

    def project(at, carry):
        where = rows_at(at * ROWS, ROWS)
        value, _ = silu_parts(mm(x_ref[where, :], w_ref[...]))
        act_ref[where, :] = value.astype(BF16)
        below = at * ROWS + lax.broadcasted_iota(jnp.int32, (ROWS, g_ref.shape[1]), 0) < length
        g_ref[where, :] = jnp.where(below, g_ref[where, :].astype(F32), 0.0).astype(BF16)
        return carry

    lax.fori_loop(0, total // ROWS, project, 0)
    half_scale = 0.5 * HEAD ** (-0.5)

    def weigh(query, keys):
        half = mm_rt(query, keys) * half_scale
        return half * (1.0 + jnp.tanh(half))

    def attend(at, carry):
        def head_cols(kind, head):
            return pl.ds(kind * width + head * HEAD, HEAD)

        heads = range(width // HEAD)
        where = rows_at(at * BLOCK, BLOCK)
        queries = [act_ref[where, head_cols(2, head)] for head in heads]

        def visit(key_at, sums):
            keys_here = rows_at(key_at * BLOCK, BLOCK)
            new = []
            for head in heads:
                weights = weigh(queries[head], act_ref[keys_here, head_cols(3, head)]).astype(BF16)
                new.append(sums[head] + mm(weights, act_ref[keys_here, head_cols(1, head)]))
            return tuple(new)

        sums = lax.fori_loop(
            0, at, visit, tuple(jnp.zeros((BLOCK, HEAD), F32) for _ in heads)
        )
        for head in heads:
            for part in range(BLOCK // ROWS):
                seen = (part + 1) * ROWS
                query = queries[head][part * ROWS : seen]
                keys_here = pl.ds(pl.multiple_of(at * BLOCK, BLOCK), seen)
                weights = weigh(query, act_ref[keys_here, head_cols(3, head)])
                ok = lax.broadcasted_iota(jnp.int32, (ROWS, seen), 1) <= (
                    part * ROWS + lax.broadcasted_iota(jnp.int32, (ROWS, seen), 0)
                )
                weights = jnp.where(ok, weights, 0.0).astype(BF16)
                att_ref[rows_at(at * BLOCK + part * ROWS, ROWS), head_cols(0, head)] = sums[head][
                    part * ROWS : seen
                ] + mm(weights, act_ref[keys_here, head_cols(1, head)])
        return carry

    lax.fori_loop(0, total // BLOCK, attend, 0)

    def measure(at, carry):
        where = rows_at(at * ROWS, ROWS)
        attended = att_ref[where, :]
        gated_grad = mm_rt(g_ref[where, :], wout_ref[...])
        t_rows = gated_grad * act_ref[where, 0:width].astype(F32)
        lane = lax.broadcasted_iota(jnp.int32, (ROWS, HEAD), 1)
        sums = jnp.zeros((ROWS, HEAD), F32)
        for at_lane, one in enumerate(
            (attended, attended * attended, t_rows, t_rows * attended)
        ):
            sums = jnp.where(lane == at_lane, jnp.sum(one, axis=1, keepdims=True), sums)
        stats_ref[:, where] = jnp.transpose(sums)[0:8, :]
        return carry

    lax.fori_loop(0, total // ROWS, measure, 0)


def backward_body(
    place_ref, x_ref, g_ref, act_ref, att_ref, stats_m_ref, stats_o_ref, w_ref, wout_ref,
    mixed_m_ref, mixed_o_ref, gx_m_ref, gx_o_ref,
    datt_ref, dgate_ref, dq_ref, dk_ref, dv_ref,
):
    mine, length = place_ref[0], place_ref[1]
    count = mixed_m_ref.shape[0]
    total, width = att_ref.shape
    hidden = 2 * width

    def middle(at, out_at, mixed_ref):
        where = rows_at(at * ROWS, ROWS)
        stats = stats_m_ref[:, where] + stats_o_ref[:, where]
        stats = jnp.transpose(
            jnp.concatenate([stats, jnp.zeros((HEAD - 8, ROWS), F32)], axis=0)
        ) * (1.0 / hidden)
        mean = stats[:, 0:1]
        inverse = lax.rsqrt(stats[:, 1:2] - mean * mean + epsilon)
        t_mean = stats[:, 2:3]
        tn_mean = inverse * (stats[:, 3:4] - mean * t_mean)
        normed = (att_ref[where, :] - mean) * inverse
        gating = act_ref[where, 0:width].astype(F32)
        gated = (normed * gating).astype(BF16)
        mixed_ref[rows_at(out_at * ROWS, ROWS), :] = mm(gated, wout_ref[...]).astype(
            mixed_ref.dtype
        )
        gated_grad = mm_rt(g_ref[where, :], wout_ref[...])
        t_rows = gated_grad * gating
        below = at * ROWS + lax.broadcasted_iota(jnp.int32, (ROWS, width), 0) < length
        datt = jnp.where(below, (t_rows - t_mean - normed * tn_mean) * inverse, 0.0)
        datt_ref[where, :] = datt.astype(BF16)
        pre = mm(x_ref[where, :], w_ref[:, 0:width])
        dgate = jnp.where(below, gated_grad * normed * slope_of(pre), 0.0)
        dgate_ref[where, :] = dgate.astype(BF16)

    def middles(at, carry):
        middle((1 - mine) * (count // ROWS) + at, at, mixed_o_ref)
        middle(mine * (count // ROWS) + at, at, mixed_m_ref)
        return carry

    lax.fori_loop(0, count // ROWS, middles, 0)
    scale = HEAD ** (-0.5)
    dq_ref[...] = jnp.zeros_like(dq_ref)

    def head_cols(kind, head):
        return pl.ds(kind * width + head * HEAD, HEAD)

    def pair(query, grad, keys, values, ok):
        scaled = mm_rt(keys, query) * scale
        value, above = silu_parts(scaled)
        weights_grad = mm_rt(values, grad)
        score_grad = weights_grad * above * (1.0 + scaled - value)
        if ok is not None:
            value = jnp.where(ok, value, 0.0)
            score_grad = jnp.where(ok, score_grad, 0.0)
        score_grad = score_grad.astype(BF16)
        return (
            mm(value.astype(BF16), grad),
            mm(score_grad, query),
            mm_lt(score_grad, keys),
        )

    def back(key_at, carry):
        heads = range(width // HEAD)
        keys_here = rows_at(key_at * BLOCK, BLOCK)
        keys = [act_ref[keys_here, head_cols(3, head)] for head in heads]
        values = [act_ref[keys_here, head_cols(1, head)] for head in heads]
        ok = lax.broadcasted_iota(jnp.int32, (BLOCK, BLOCK), 0) <= (
            lax.broadcasted_iota(jnp.int32, (BLOCK, BLOCK), 1)
        )

        def visit(at, sums, ok=None):
            where = rows_at(at * BLOCK, BLOCK)
            new = []
            for head in heads:
                more_v, more_k, more_q = pair(
                    act_ref[where, head_cols(2, head)],
                    datt_ref[where, head_cols(0, head)],
                    keys[head],
                    values[head],
                    ok,
                )
                dq_ref[where, head_cols(0, head)] += more_q
                new += [sums[2 * head] + more_v, sums[2 * head + 1] + more_k]
            return tuple(new)

        zero = tuple(jnp.zeros((BLOCK, HEAD), F32) for _ in range(2 * len(heads)))
        sums = visit(key_at, zero, ok)
        sums = lax.fori_loop(key_at + 1, total // BLOCK, visit, sums)
        for head in heads:
            dv_ref[keys_here, head_cols(0, head)] = sums[2 * head]
            dk_ref[keys_here, head_cols(0, head)] = sums[2 * head + 1]
        return carry

    lax.fori_loop(0, total // BLOCK, back, 0)

    def finish(at, out_at, gx_ref):
        where = rows_at(at * ROWS, ROWS)
        slope = slope_of(mm(x_ref[where, :], w_ref[:, width:]))
        factor = 0.5 * scale
        grads = jnp.concatenate(
            [
                dgate_ref[where, :],
                (dv_ref[where, :] * slope[:, 0:width]).astype(BF16),
                (dq_ref[where, :] * factor * slope[:, width : 2 * width]).astype(BF16),
                (dk_ref[where, :] * factor * slope[:, 2 * width :]).astype(BF16),
            ],
            axis=1,
        )
        gx_ref[rows_at(out_at * ROWS, ROWS), :] = mm_rt(grads, w_ref[...]).astype(gx_ref.dtype)

    def finishes(at, carry):
        finish((1 - mine) * (count // ROWS) + at, at, gx_o_ref)
        finish(mine * (count // ROWS) + at, at, gx_m_ref)
        return carry

    lax.fori_loop(0, count // ROWS, finishes, 0)


def scatter_body(place_ref, slots_ref, embedded_ref, g_ref, gx_m_ref, gx_o_ref, out_ref, grads, hot):
    count = embedded_ref.shape[0]
    first = place_ref[0] * count

    def embed_back(at, carry):
        where = rows_at(at * ROWS, ROWS)
        normed, inverse = normalize(embedded_ref[where, :])
        grad_x = gx_m_ref[where, :].astype(F32) + gx_o_ref[where, :].astype(F32)
        back = (
            grad_x
            - jnp.mean(grad_x, axis=-1, keepdims=True)
            - normed * jnp.mean(grad_x * normed, axis=-1, keepdims=True)
        ) * inverse
        below = (
            first + at * ROWS + lax.broadcasted_iota(jnp.int32, back.shape, 0) < place_ref[1]
        )
        grads[where, :] = jnp.where(below, g_ref[where, :].astype(F32) + back, 0.0).astype(BF16)
        return carry

    lax.fori_loop(0, count // ROWS, embed_back, 0)
    places = lax.broadcasted_iota(jnp.int32, (ROWS, HEAD), 0)

    def step(at, carry):
        here = places + at * ROWS
        for part in range(count // HEAD):
            cols = slice(part * HEAD, (part + 1) * HEAD)
            total = jnp.zeros((ROWS, HEAD), F32)
            for feature in range(slots_ref.shape[0]):
                total = total + jnp.where(slots_ref[feature : feature + 1, cols] == here, 1.0, 0.0)
            hot[:, cols] = total.astype(BF16)
        out_ref[rows_at(at * ROWS, ROWS), :] = mm(hot[...], grads[...]).astype(BF16)
        return carry

    lax.fori_loop(0, out_ref.shape[0] // ROWS, step, 0)


def owner_body(place_ref, ids_ref, returned_ref, mine_ref, other_ref, hot):
    count = mine_ref.shape[0]
    places = lax.broadcasted_iota(jnp.int32, (ROWS, HEAD), 0)

    def rows_of(at, out_at, out_ref):
        here = places + at * ROWS
        for part in range(ids_ref.shape[0] * ids_ref.shape[1] // HEAD):
            row, col = divmod(part * HEAD, ids_ref.shape[1])
            hit = ids_ref[row : row + 1, col : col + HEAD] == here
            hot[:, part * HEAD : (part + 1) * HEAD] = jnp.where(hit, 1.0, 0.0).astype(BF16)
        out_ref[rows_at(out_at * ROWS, ROWS), :] = mm(hot[...], returned_ref[...]).astype(
            out_ref.dtype
        )

    def step(at, carry):
        rows_of((1 - place_ref[0]) * (count // ROWS) + at, at, other_ref)
        rows_of(place_ref[0] * (count // ROWS) + at, at, mine_ref)
        return carry

    lax.fori_loop(0, count // ROWS, step, 0)


def swap(array):
    return lax.ppermute(array, "ctx", [(0, 1), (1, 0)])


def on_device(item_table, serve_rows, token_slots, lengths, w_proj, w_out, grad_out):
    table_rows, row_width = item_table.shape
    requesters, asked = serve_rows.shape
    slot_total = requesters * asked
    row_count, features = token_slots.shape[1:]
    hidden_full = w_out.shape[0]
    shards = lax.axis_size("ctx")
    assert shards == 2
    total = row_count * shards
    mine = lax.axis_index("ctx")
    place = jnp.stack([mine, lengths[0]])
    shape = jax.ShapeDtypeStruct

    cotangent = grad_out[0]
    cotangent_o = swap(cotangent)
    ids = serve_rows.reshape(-1, BLOCK)
    served = call(
        serve_body,
        shape((slot_total, row_width), BF16),
        [vmem(), vmem()],
        [pltpu.VMEM((table_rows, row_width), BF16), pltpu.VMEM((BLOCK, table_rows), BF16)],
        flops=2 * slot_total * table_rows * row_width,
        moved=4 * table_rows * row_width,
    )(ids, item_table)
    fetched = lax.all_to_all(
        served.reshape(requesters, asked, row_width),
        "table",
        split_axis=0,
        concat_axis=0,
        tiled=True,
    ).reshape(slot_total, row_width)
    slots = token_slots[0].T
    embedded, normed = call(
        embed_body,
        (shape((row_count, row_width), F32), shape((row_count, row_width), BF16)),
        [vmem(), vmem()],
        [pltpu.VMEM((ROWS, slot_total), BF16)],
        flops=2 * slot_total * row_count * row_width,
        moved=2 * slot_total * row_width,
    )(slots, fetched)

    head_total = hidden_full // HEAD
    share = head_total // shards
    width = share * HEAD
    proj_cols = lax.dynamic_slice_in_dim(
        w_proj.reshape(row_width, 4, head_total, HEAD), mine * share, share, 2
    ).reshape(row_width, 4 * width)
    out_rows = lax.dynamic_slice_in_dim(
        w_out.reshape(head_total, HEAD, row_width), mine * share, share, 0
    ).reshape(width, row_width)

    normed_o = swap(normed)
    x_all, g_all, act, attended, stats = call(
        forward_body,
        (
            shape((total, row_width), BF16),
            shape((total, row_width), BF16),
            shape((total, 4 * width), BF16),
            shape((total, width), F32),
            shape((8, total), F32),
        ),
        [smem()] + [vmem()] * 6,
        flops=2 * total * total * width + 8 * total * row_width * width,
        moved=12 * total * width,
    )(place, normed, normed_o, cotangent, cotangent_o, proj_cols, out_rows)
    stats_o = swap(stats)
    part = shape((row_count, row_width), BF16)
    mixed_m, mixed_o, gx_m, gx_o = call(
        backward_body,
        (shape((row_count, row_width), F32), part, shape((row_count, row_width), F32), part),
        [smem()] + [vmem()] * 8,
        [
            pltpu.VMEM((total, width), BF16),
            pltpu.VMEM((total, width), BF16),
            pltpu.VMEM((total, width), F32),
            pltpu.VMEM((total, width), F32),
            pltpu.VMEM((total, width), F32),
        ],
        flops=5 * total * total * width + 16 * total * row_width * width,
        moved=12 * total * width,
    )(place, x_all, g_all, act, attended, stats, stats_o, proj_cols, out_rows)
    gx_in = swap(gx_o)
    mixed_in = swap(mixed_o)
    slot_grads = call(
        scatter_body,
        shape((slot_total, row_width), BF16),
        [smem()] + [vmem()] * 5,
        [pltpu.VMEM((row_count, row_width), BF16), pltpu.VMEM((ROWS, row_count), BF16)],
        flops=2 * slot_total * row_count * row_width,
        moved=2 * slot_total * row_width,
    )(place, slots, embedded, cotangent, gx_m, gx_in)
    returned = lax.all_to_all(
        slot_grads.reshape(requesters, asked, row_width),
        "table",
        split_axis=0,
        concat_axis=0,
        tiled=True,
    ).reshape(slot_total, row_width)
    half_rows = table_rows // shards
    owner_m, owner_o = call(
        owner_body,
        (shape((half_rows, row_width), F32), shape((half_rows, row_width), BF16)),
        [smem()] + [vmem()] * 2,
        [pltpu.VMEM((ROWS, slot_total), BF16)],
        flops=2 * slot_total * table_rows * row_width,
        moved=2 * slot_total * row_width,
    )(place, ids, returned)
    grad_table = owner_m + swap(owner_o).astype(F32)
    positions = mine * row_count + jnp.arange(row_count, dtype=jnp.int32)
    layer_out = jnp.where(
        (positions < lengths[0])[:, None], embedded + (mixed_m + mixed_in.astype(F32)), 0.0
    ).astype(BF16)
    return (layer_out[None], grad_table)


def solution(mesh):
    placed = (
        P("table", None),
        P("table", "ctx"),
        P("table", "ctx", None),
        P("table"),
        P(),
        P(),
        P("table", "ctx", None),
    )
    return jax.shard_map(
        on_device,
        mesh=mesh,
        in_specs=placed,
        out_specs=(P("table", "ctx", None), P(("table", "ctx"), None)),
        check_vma=False,
    )
```

```python
import functools

import jax
import jax.numpy as jnp
from jax import lax
from jax.experimental import pallas as pl
from jax.experimental.pallas import tpu as pltpu
from jax.sharding import PartitionSpec as P

HEAD = 128
epsilon = 1e-05
F32 = jnp.float32
BF16 = jnp.bfloat16
ROWS = 256
BLOCK = 512
SENDS = (1, 3, 4, 8)
RECEIVES = (5, 4, 4, 3)


def mm(lhs, rhs):
    return lax.dot_general(lhs, rhs, (((1,), (0,)), ((), ())), preferred_element_type=F32)


def mm_rt(lhs, rhs):
    return lax.dot_general(lhs, rhs, (((1,), (1,)), ((), ())), preferred_element_type=F32)


def mm_lt(lhs, rhs):
    return lax.dot_general(lhs, rhs, (((0,), (0,)), ((), ())), preferred_element_type=F32)


def rows_at(start, count):
    return pl.ds(pl.multiple_of(start, count), count)


def vmem():
    return pl.BlockSpec(memory_space=pltpu.VMEM)


def smem():
    return pl.BlockSpec(memory_space=pltpu.SMEM)


def call(body, out_shape, in_specs, scratch=(), flops=0, moved=0):
    return pl.pallas_call(
        body,
        out_shape=out_shape,
        in_specs=in_specs,
        out_specs=jax.tree.map(lambda _: vmem(), out_shape),
        scratch_shapes=list(scratch),
        compiler_params=pltpu.CompilerParams(vmem_limit_bytes=60 * 1024 * 1024),
        cost_estimate=pl.CostEstimate(flops=flops, bytes_accessed=moved, transcendentals=0),
    )


def column(row, count):
    return jnp.transpose(jnp.broadcast_to(row, (HEAD, count)))


def piece_ids(piece_starts, asked, part):
    lane = lax.broadcasted_iota(jnp.int32, (1, HEAD), 1)
    first = part * HEAD // asked
    here = lane + (piece_starts[first] + part * HEAD - first * asked)
    for piece in range(first + 1, (part + 1) * HEAD // asked + (1 if asked > HEAD else 0)):
        begin = piece * asked - part * HEAD
        if begin < HEAD:
            here = jnp.where(lane >= begin, lane + (piece_starts[piece] - begin), here)
    return here


def serve_body(partners, cast, place_ref, ids_ref, table_ref, *refs):
    outs, hot = refs[: len(partners)], refs[-1]
    if cast:
        low_ref = refs[len(partners)]
        low_ref[...] = table_ref[...].astype(BF16)
    else:
        low_ref = table_ref
    asked = ids_ref.shape[1]
    lanes = lax.broadcasted_iota(jnp.int32, (asked, HEAD), 1)
    for partner, out_ref in zip(partners, outs):
        ids = column(ids_ref[pl.ds(place_ref[2] ^ partner, 1), :], asked)
        for part in range(table_ref.shape[0] // HEAD):
            hit = ids == lanes + part * HEAD
            hot[:, part * HEAD : (part + 1) * HEAD] = jnp.where(hit, 1.0, 0.0).astype(BF16)
        out_ref[...] = mm(hot[...], low_ref[...]).astype(BF16)


def embed_body(partners, first, last, asked, place_ref, slots_ref, *refs):
    refs = list(refs)
    chunks = [refs.pop(0) for _ in partners]
    sums_in = None if first else refs.pop(0)
    sums_out = refs.pop(0)
    normed_ref = refs.pop(0) if last else None
    rows_ref, hot = refs
    starts = [(place_ref[2] ^ partner) * asked for partner in partners]
    for at, chunk in enumerate(chunks):
        rows_ref[at * asked : (at + 1) * asked, :] = chunk[...]

    def step(at, carry):
        where = rows_at(at * ROWS, ROWS)
        ids = [
            column(slots_ref[feature : feature + 1, where], ROWS)
            for feature in range(slots_ref.shape[0])
        ]
        for part in range(len(partners) * asked // HEAD):
            here = piece_ids(starts, asked, part)
            count = jnp.where(ids[0] == here, 1.0, 0.0)
            for one in ids[1:]:
                count = count + jnp.where(one == here, 1.0, 0.0)
            hot[:, part * HEAD : (part + 1) * HEAD] = count.astype(BF16)
        value = mm(hot[...], rows_ref[...])
        if not first:
            value = value + sums_in[where, :]
        sums_out[where, :] = value
        if last:
            normed_ref[where, :] = normalize(value)[0].astype(BF16)
        return carry

    lax.fori_loop(0, sums_out.shape[0] // ROWS, step, 0)


def normalize(inputs):
    centred = inputs - jnp.mean(inputs, axis=-1, keepdims=True)
    inverse = lax.rsqrt(jnp.mean(centred * centred, axis=-1, keepdims=True) + epsilon)
    return (centred * inverse, inverse)


def silu_parts(inputs):
    half = inputs * 0.5
    above = 1.0 + jnp.tanh(half)
    value = half * above
    return value, above


def slope_of(inputs):
    value, above = silu_parts(inputs)
    return 0.5 * above * (1.0 + inputs - value)


def weight(w_ref, kind, mine, width):
    return w_ref[:, pl.ds(pl.multiple_of((2 * kind + mine) * width, width), width)]


def forward_body(
    place_ref, xm_ref, xo_ref, gm_ref, go_ref, w_ref, wout_ref,
    x_ref, g_ref, act_ref, att_ref, stats_ref,
):
    mine, length = place_ref[0], place_ref[1]
    count = xm_ref.shape[0]
    total = x_ref.shape[0]
    width = att_ref.shape[1]
    x_ref[rows_at(mine * count, count), :] = xm_ref[...]
    x_ref[rows_at((1 - mine) * count, count), :] = xo_ref[...]
    g_ref[rows_at(mine * count, count), :] = gm_ref[...]
    g_ref[rows_at((1 - mine) * count, count), :] = go_ref[...]

    def project(at, carry):
        where = rows_at(at * ROWS, ROWS)
        for kind in range(4):
            value, _ = silu_parts(mm(x_ref[where, :], weight(w_ref, kind, mine, width)))
            act_ref[where, kind * width : (kind + 1) * width] = value.astype(BF16)
        below = at * ROWS + lax.broadcasted_iota(jnp.int32, (ROWS, g_ref.shape[1]), 0) < length
        g_ref[where, :] = jnp.where(below, g_ref[where, :].astype(F32), 0.0).astype(BF16)
        return carry

    lax.fori_loop(0, total // ROWS, project, 0)
    half_scale = 0.5 * HEAD ** (-0.5)

    def weigh(query, keys):
        half = mm_rt(query, keys) * half_scale
        return half * (1.0 + jnp.tanh(half))

    def attend(at, carry):
        def head_cols(kind, head):
            return pl.ds(kind * width + head * HEAD, HEAD)

        heads = range(width // HEAD)
        where = rows_at(at * BLOCK, BLOCK)
        queries = [act_ref[where, head_cols(2, head)] for head in heads]

        def visit(key_at, sums):
            keys_here = rows_at(key_at * BLOCK, BLOCK)
            new = []
            for head in heads:
                weights = weigh(queries[head], act_ref[keys_here, head_cols(3, head)]).astype(BF16)
                new.append(sums[head] + mm(weights, act_ref[keys_here, head_cols(1, head)]))
            return tuple(new)

        sums = lax.fori_loop(
            0, at, visit, tuple(jnp.zeros((BLOCK, HEAD), F32) for _ in heads)
        )
        for head in heads:
            for part in range(BLOCK // ROWS):
                seen = (part + 1) * ROWS
                query = queries[head][part * ROWS : seen]
                keys_here = pl.ds(pl.multiple_of(at * BLOCK, BLOCK), seen)
                weights = weigh(query, act_ref[keys_here, head_cols(3, head)])
                ok = lax.broadcasted_iota(jnp.int32, (ROWS, seen), 1) <= (
                    part * ROWS + lax.broadcasted_iota(jnp.int32, (ROWS, seen), 0)
                )
                weights = jnp.where(ok, weights, 0.0).astype(BF16)
                att_ref[rows_at(at * BLOCK + part * ROWS, ROWS), head_cols(0, head)] = sums[head][
                    part * ROWS : seen
                ] + mm(weights, act_ref[keys_here, head_cols(1, head)])
        return carry

    lax.fori_loop(0, total // BLOCK, attend, 0)

    def measure(at, carry):
        where = rows_at(at * ROWS, ROWS)
        attended = att_ref[where, :]
        gated_grad = mm_rt(g_ref[where, :], wout_ref[rows_at(mine * width, width), :])
        t_rows = gated_grad * act_ref[where, 0:width].astype(F32)
        lane = lax.broadcasted_iota(jnp.int32, (ROWS, HEAD), 1)
        sums = jnp.zeros((ROWS, HEAD), F32)
        for at_lane, one in enumerate(
            (attended, attended * attended, t_rows, t_rows * attended)
        ):
            sums = jnp.where(lane == at_lane, jnp.sum(one, axis=1, keepdims=True), sums)
        stats_ref[:, where] = jnp.transpose(sums)[0:8, :]
        return carry

    lax.fori_loop(0, total // ROWS, measure, 0)


def backward_body(
    place_ref, x_ref, g_ref, act_ref, att_ref, stats_m_ref, stats_o_ref, w_ref, wout_ref,
    mixed_m_ref, mixed_o_ref, gx_m_ref, gx_o_ref,
    datt_ref, dgate_ref, dq_ref, dk_ref, dv_ref,
):
    mine, length = place_ref[0], place_ref[1]
    count = mixed_m_ref.shape[0]
    total, width = att_ref.shape
    hidden = 2 * width

    def middle(at, out_at, mixed_ref):
        where = rows_at(at * ROWS, ROWS)
        stats = stats_m_ref[:, where] + stats_o_ref[:, where]
        stats = jnp.transpose(
            jnp.concatenate([stats, jnp.zeros((HEAD - 8, ROWS), F32)], axis=0)
        ) * (1.0 / hidden)
        mean = stats[:, 0:1]
        inverse = lax.rsqrt(stats[:, 1:2] - mean * mean + epsilon)
        t_mean = stats[:, 2:3]
        tn_mean = inverse * (stats[:, 3:4] - mean * t_mean)
        normed = (att_ref[where, :] - mean) * inverse
        gating = act_ref[where, 0:width].astype(F32)
        gated = (normed * gating).astype(BF16)
        mixed_ref[rows_at(out_at * ROWS, ROWS), :] = mm(gated, wout_ref[rows_at(mine * width, width), :]).astype(
            mixed_ref.dtype
        )
        gated_grad = mm_rt(g_ref[where, :], wout_ref[rows_at(mine * width, width), :])
        t_rows = gated_grad * gating
        below = at * ROWS + lax.broadcasted_iota(jnp.int32, (ROWS, width), 0) < length
        datt = jnp.where(below, (t_rows - t_mean - normed * tn_mean) * inverse, 0.0)
        datt_ref[where, :] = datt.astype(BF16)
        pre = mm(x_ref[where, :], weight(w_ref, 0, mine, width))
        dgate = jnp.where(below, gated_grad * normed * slope_of(pre), 0.0)
        dgate_ref[where, :] = dgate.astype(BF16)

    def middles(at, carry):
        middle((1 - mine) * (count // ROWS) + at, at, mixed_o_ref)
        middle(mine * (count // ROWS) + at, at, mixed_m_ref)
        return carry

    lax.fori_loop(0, count // ROWS, middles, 0)
    scale = HEAD ** (-0.5)
    dq_ref[...] = jnp.zeros_like(dq_ref)

    def head_cols(kind, head):
        return pl.ds(kind * width + head * HEAD, HEAD)

    def pair(query, grad, keys, values, ok):
        scaled = mm_rt(keys, query) * scale
        value, above = silu_parts(scaled)
        weights_grad = mm_rt(values, grad)
        score_grad = weights_grad * above * (1.0 + scaled - value)
        if ok is not None:
            value = jnp.where(ok, value, 0.0)
            score_grad = jnp.where(ok, score_grad, 0.0)
        score_grad = score_grad.astype(BF16)
        return (
            mm(value.astype(BF16), grad),
            mm(score_grad, query),
            mm_lt(score_grad, keys),
        )

    def back(key_at, carry):
        heads = range(width // HEAD)
        keys_here = rows_at(key_at * BLOCK, BLOCK)
        keys = [act_ref[keys_here, head_cols(3, head)] for head in heads]
        values = [act_ref[keys_here, head_cols(1, head)] for head in heads]
        ok = lax.broadcasted_iota(jnp.int32, (BLOCK, BLOCK), 0) <= (
            lax.broadcasted_iota(jnp.int32, (BLOCK, BLOCK), 1)
        )

        def visit(at, sums, ok=None):
            where = rows_at(at * BLOCK, BLOCK)
            new = []
            for head in heads:
                more_v, more_k, more_q = pair(
                    act_ref[where, head_cols(2, head)],
                    datt_ref[where, head_cols(0, head)],
                    keys[head],
                    values[head],
                    ok,
                )
                dq_ref[where, head_cols(0, head)] += more_q
                new += [sums[2 * head] + more_v, sums[2 * head + 1] + more_k]
            return tuple(new)

        zero = tuple(jnp.zeros((BLOCK, HEAD), F32) for _ in range(2 * len(heads)))
        sums = visit(key_at, zero, ok)
        sums = lax.fori_loop(key_at + 1, total // BLOCK, visit, sums)
        for head in heads:
            dv_ref[keys_here, head_cols(0, head)] = sums[2 * head]
            dk_ref[keys_here, head_cols(0, head)] = sums[2 * head + 1]
        return carry

    lax.fori_loop(0, total // BLOCK, back, 0)

    def finish(at, out_at, gx_ref):
        where = rows_at(at * ROWS, ROWS)
        total_x = mm_rt(dgate_ref[where, :], weight(w_ref, 0, mine, width))
        for kind, grad_ref, factor in (
            (1, dv_ref, 1.0), (2, dq_ref, 0.5 * scale), (3, dk_ref, 0.5 * scale)
        ):
            columns = weight(w_ref, kind, mine, width)
            slope = slope_of(mm(x_ref[where, :], columns))
            grad = (grad_ref[where, :] * (factor * slope)).astype(BF16)
            total_x = total_x + mm_rt(grad, columns)
        gx_ref[rows_at(out_at * ROWS, ROWS), :] = total_x.astype(gx_ref.dtype)

    def finishes(at, carry):
        finish((1 - mine) * (count // ROWS) + at, at, gx_o_ref)
        finish(mine * (count // ROWS) + at, at, gx_m_ref)
        return carry

    lax.fori_loop(0, count // ROWS, finishes, 0)


def embed_back(place_ref, embedded_ref, g_ref, gx_m_ref, gx_o_ref, grads):
    count = embedded_ref.shape[0]
    first = place_ref[0] * count

    def step(at, carry):
        where = rows_at(at * ROWS, ROWS)
        normed, inverse = normalize(embedded_ref[where, :])
        grad_x = gx_m_ref[where, :].astype(F32) + gx_o_ref[where, :].astype(F32)
        back = (
            grad_x
            - jnp.mean(grad_x, axis=-1, keepdims=True)
            - normed * jnp.mean(grad_x * normed, axis=-1, keepdims=True)
        ) * inverse
        below = (
            first + at * ROWS + lax.broadcasted_iota(jnp.int32, back.shape, 0) < place_ref[1]
        )
        grads[where, :] = jnp.where(below, g_ref[where, :].astype(F32) + back, 0.0).astype(BF16)
        return carry

    lax.fori_loop(0, count // ROWS, step, 0)


def scatter_body(partners, first, asked, place_ref, slots_ref, *refs):
    refs = list(refs)
    if first:
        parts = [refs.pop(0) for _ in range(4)]
    else:
        grads = refs.pop(0)
    outs = [refs.pop(0) for _ in partners]
    if first:
        grads = refs.pop(0)
        embed_back(place_ref, *parts, grads)
    hot = refs.pop(0)
    count = grads.shape[0]
    places = lax.broadcasted_iota(jnp.int32, (asked, HEAD), 0)
    for partner, out_ref in zip(partners, outs):
        here = places + (place_ref[2] ^ partner) * asked
        for part in range(count // HEAD):
            cols = slice(part * HEAD, (part + 1) * HEAD)
            total = jnp.zeros((asked, HEAD), F32)
            for feature in range(slots_ref.shape[0]):
                total = total + jnp.where(slots_ref[feature : feature + 1, cols] == here, 1.0, 0.0)
            hot[:, cols] = total.astype(BF16)
        out_ref[...] = mm(hot[...], grads[...]).astype(BF16)


def owner_body(partners, first, last, place_ref, ids_ref, *refs):
    refs = list(refs)
    chunks = [refs.pop(0) for _ in partners]
    sums_in = None if first else refs.pop(0)
    if last:
        mine_ref, other_ref = refs.pop(0), refs.pop(0)
        table_rows = 2 * mine_ref.shape[0]
    else:
        sums_out = refs.pop(0)
        table_rows = sums_out.shape[0]
    rows_ref, hot = refs
    asked = ids_ref.shape[1]
    for at, chunk in enumerate(chunks):
        rows_ref[at * asked : (at + 1) * asked, :] = chunk[...]
    ids = jnp.concatenate(
        [ids_ref[pl.ds(place_ref[2] ^ partner, 1), :] for partner in partners], axis=1
    )
    places = lax.broadcasted_iota(jnp.int32, (ROWS, HEAD), 0)

    def rows_of(at):
        here = places + at * ROWS
        for part in range(len(partners) * asked // HEAD):
            cols = slice(part * HEAD, (part + 1) * HEAD)
            hot[:, cols] = jnp.where(ids[:, cols] == here, 1.0, 0.0).astype(BF16)
        value = mm(hot[...], rows_ref[...])
        if not first:
            value = value + sums_in[rows_at(at * ROWS, ROWS), :]
        return value

    half = table_rows // 2 // ROWS

    def step(at, carry):
        if last:
            other_ref[rows_at(at * ROWS, ROWS), :] = rows_of(
                (1 - place_ref[0]) * half + at
            ).astype(BF16)
            mine_ref[rows_at(at * ROWS, ROWS), :] = rows_of(place_ref[0] * half + at)
        else:
            for offset in range(2):
                now = 2 * at + offset
                sums_out[rows_at(now * ROWS, ROWS), :] = rows_of(now)
        return carry

    lax.fori_loop(0, half, step, 0)


def split(items, shares):
    total, groups, begin = sum(shares), [], 0
    for at in range(len(shares)):
        end = len(items) * sum(shares[: at + 1]) // total
        groups.append(items[begin:end])
        begin = end
    return groups


def swap(array):
    return lax.ppermute(array, "ctx", [(0, 1), (1, 0)])


def on_device(item_table, serve_rows, token_slots, lengths, w_proj, w_out, grad_out):
    table_rows, row_width = item_table.shape
    requesters, asked = serve_rows.shape
    row_count, features = token_slots.shape[1:]
    hidden_full = w_out.shape[0]
    assert lax.axis_size("ctx") == 2 and requesters & (requesters - 1) == 0
    total = row_count * 2
    width = hidden_full // 2
    mine = lax.axis_index("ctx")
    me = lax.axis_index("table")
    place = jnp.stack([mine, lengths[0], me])
    shape = jax.ShapeDtypeStruct
    chunk = shape((asked, row_width), BF16)
    far_first = list(range(requesters - 1, 0, -1))

    def cross(array, partner):
        return lax.ppermute(
            array, "table", [(one, one ^ partner) for one in range(requesters)]
        )

    cotangent = grad_out[0]
    cotangent_o = swap(cotangent)
    slots = token_slots[0].T
    fetched = {}
    table_low = item_table
    for at, group in enumerate(split(far_first + [0], SENDS)):
        outs = [chunk] * len(group)
        if at == 0:
            outs.append(shape((table_rows, row_width), BF16))
        served = call(
            functools.partial(serve_body, tuple(group), at == 0),
            tuple(outs),
            [smem()] + [vmem()] * 2,
            [pltpu.VMEM((asked, table_rows), BF16)],
            flops=2 * len(group) * asked * table_rows * row_width,
            moved=2 * table_rows * row_width,
        )(place, serve_rows, table_low)
        if at == 0:
            table_low = served[-1]
        for partner, rows in zip(group, served):
            fetched[partner] = cross(rows, partner) if partner else rows

    sums = None
    groups = split([0] + far_first, RECEIVES)
    for at, group in enumerate(groups):
        first, last = at == 0, at == len(groups) - 1
        outs = [shape((row_count, row_width), F32)]
        if last:
            outs.append(shape((row_count, row_width), BF16))
        made = call(
            functools.partial(embed_body, tuple(group), first, last, asked),
            tuple(outs),
            [smem()] + [vmem()] * (1 + len(group) + (not first)),
            [
                pltpu.VMEM((len(group) * asked, row_width), BF16),
                pltpu.VMEM((ROWS, len(group) * asked), BF16),
            ],
            flops=2 * len(group) * asked * row_count * row_width,
            moved=8 * row_count * row_width,
        )(place, slots, *[fetched[one] for one in group], *([] if first else [sums]))
        sums = made[0]
    embedded, normed = made

    normed_o = swap(normed)
    x_all, g_all, act, attended, stats = call(
        forward_body,
        (
            shape((total, row_width), BF16),
            shape((total, row_width), BF16),
            shape((total, 4 * width), BF16),
            shape((total, width), F32),
            shape((8, total), F32),
        ),
        [smem()] + [vmem()] * 6,
        flops=2 * total * total * width + 8 * total * row_width * width,
        moved=12 * total * width,
    )(place, normed, normed_o, cotangent, cotangent_o, w_proj, w_out)
    stats_o = swap(stats)
    part = shape((row_count, row_width), BF16)
    mixed_m, mixed_o, gx_m, gx_o = call(
        backward_body,
        (shape((row_count, row_width), F32), part, shape((row_count, row_width), F32), part),
        [smem()] + [vmem()] * 8,
        [
            pltpu.VMEM((total, width), BF16),
            pltpu.VMEM((total, width), BF16),
            pltpu.VMEM((total, width), F32),
            pltpu.VMEM((total, width), F32),
            pltpu.VMEM((total, width), F32),
        ],
        flops=5 * total * total * width + 16 * total * row_width * width,
        moved=12 * total * width,
    )(place, x_all, g_all, act, attended, stats, stats_o, w_proj, w_out)
    gx_in = swap(gx_o)
    mixed_in = swap(mixed_o)

    returned = {}
    grads = None
    for at, group in enumerate(split(far_first + [0], SENDS)):
        outs = [chunk] * len(group)
        operands = [grads]
        if at == 0:
            outs.append(shape((row_count, row_width), BF16))
            operands = [embedded, cotangent, gx_m, gx_in]
        made = call(
            functools.partial(scatter_body, tuple(group), at == 0, asked),
            tuple(outs),
            [smem()] + [vmem()] * (1 + len(operands)),
            [pltpu.VMEM((asked, row_count), BF16)],
            flops=2 * len(group) * asked * row_count * row_width,
            moved=2 * len(group) * asked * row_width,
        )(place, slots, *operands)
        if at == 0:
            grads = made[-1]
        for partner, rows in zip(group, made):
            returned[partner] = cross(rows, partner) if partner else rows

    half_rows = table_rows // 2
    for at, group in enumerate(groups):
        first, last = at == 0, at == len(groups) - 1
        if last:
            outs = (shape((half_rows, row_width), F32), shape((half_rows, row_width), BF16))
        else:
            outs = (shape((table_rows, row_width), F32),)
        made = call(
            functools.partial(owner_body, tuple(group), first, last),
            outs,
            [smem()] + [vmem()] * (1 + len(group) + (not first)),
            [
                pltpu.VMEM((len(group) * asked, row_width), BF16),
                pltpu.VMEM((ROWS, len(group) * asked), BF16),
            ],
            flops=2 * len(group) * asked * table_rows * row_width,
            moved=8 * table_rows * row_width,
        )(place, serve_rows, *[returned[one] for one in group], *([] if first else [sums]))
        sums = made[0]
    owner_m, owner_o = made
    grad_table = owner_m + swap(owner_o).astype(F32)
    positions = mine * row_count + jnp.arange(row_count, dtype=jnp.int32)
    layer_out = jnp.where(
        (positions < lengths[0])[:, None], embedded + (mixed_m + mixed_in.astype(F32)), 0.0
    ).astype(BF16)
    return (layer_out[None], grad_table)


def solution(mesh):
    placed = (
        P("table", None),
        P("table", "ctx"),
        P("table", "ctx", None),
        P("table"),
        P(),
        P(),
        P("table", "ctx", None),
    )
    return jax.shard_map(
        on_device,
        mesh=mesh,
        in_specs=placed,
        out_specs=(P("table", "ctx", None), P(("table", "ctx"), None)),
        check_vma=False,
    )
```

```python
import functools

import jax
import jax.numpy as jnp
from jax import lax
from jax.experimental import pallas as pl
from jax.experimental.pallas import tpu as pltpu
from jax.sharding import PartitionSpec as P

HEAD = 128
epsilon = 1e-05
F32 = jnp.float32
BF16 = jnp.bfloat16
I16 = jnp.int16
ROWS = 256
BLOCK = 512
SENDS = (1, 3, 5, 7)
RECEIVES = (8, 5, 3)


def mm(lhs, rhs):
    return lax.dot_general(lhs, rhs, (((1,), (0,)), ((), ())), preferred_element_type=F32)


def mm_rt(lhs, rhs):
    return lax.dot_general(lhs, rhs, (((1,), (1,)), ((), ())), preferred_element_type=F32)


def mm_lt(lhs, rhs):
    return lax.dot_general(lhs, rhs, (((0,), (0,)), ((), ())), preferred_element_type=F32)


def rows_at(start, count):
    return pl.ds(pl.multiple_of(start, count), count)


def vmem():
    return pl.BlockSpec(memory_space=pltpu.VMEM)


def smem():
    return pl.BlockSpec(memory_space=pltpu.SMEM)


def call(body, out_shape, in_specs, scratch=(), flops=0, moved=0):
    return pl.pallas_call(
        body,
        out_shape=out_shape,
        in_specs=in_specs,
        out_specs=jax.tree.map(lambda _: vmem(), out_shape),
        scratch_shapes=list(scratch),
        compiler_params=pltpu.CompilerParams(vmem_limit_bytes=60 * 1024 * 1024),
        cost_estimate=pl.CostEstimate(flops=flops, bytes_accessed=moved, transcendentals=0),
    )


def column(row, count):
    return jnp.transpose(jnp.broadcast_to(row, (HEAD, count))).astype(I16)


def hits(ids, here):
    return jnp.where(ids == here, jnp.ones((), BF16), jnp.zeros((), BF16))


def hit_counts(all_ids, here):
    found = [hits(ids, here) for ids in all_ids]
    while len(found) > 1:
        found = [sum(found[at : at + 2][1:], found[at]) for at in range(0, len(found), 2)]
    return found[0]


def piece_ids(piece_starts, asked, part):
    lane = lax.broadcasted_iota(jnp.int32, (1, HEAD), 1)
    first = part * HEAD // asked
    here = lane + (piece_starts[first] + part * HEAD - first * asked)
    for piece in range(first + 1, -(-(part + 1) * HEAD // asked)):
        begin = piece * asked - part * HEAD
        here = jnp.where(lane >= begin, lane + (piece_starts[piece] - begin), here)
    return here


def serve_body(partners, cast, place_ref, ids_ref, table_ref, *refs):
    outs, hot = refs[: len(partners)], refs[-1]
    if cast:
        low_ref = refs[len(partners)]
        low_ref[...] = table_ref[...].astype(BF16)
    else:
        low_ref = table_ref
    asked = ids_ref.shape[1]
    lanes = lax.broadcasted_iota(jnp.int32, (asked, HEAD), 1).astype(I16)
    for at, partner in enumerate(partners):
        ids = column(ids_ref[pl.ds(place_ref[2] ^ partner, 1), :], asked)
        for part in range(table_ref.shape[0] // HEAD):
            hot[at * asked : (at + 1) * asked, part * HEAD : (part + 1) * HEAD] = hits(
                ids, lanes + jnp.int16(part * HEAD)
            )
    rows = mm(hot[...], low_ref[...]).astype(BF16)
    for at, out_ref in enumerate(outs):
        out_ref[...] = rows[at * asked : (at + 1) * asked, :]


def embed_body(partners, first, last, asked, place_ref, slots_ref, *refs):
    refs = list(refs)
    chunks = [refs.pop(0) for _ in partners]
    sums_in = None if first else refs.pop(0)
    sums_out = refs.pop(0)
    normed_ref = refs.pop(0) if last else None
    rows_ref, hot = refs
    starts = [(place_ref[2] ^ partner) * asked for partner in partners]
    for at, chunk in enumerate(chunks):
        rows_ref[at * asked : (at + 1) * asked, :] = chunk[...]

    def step(at, carry):
        where = rows_at(at * ROWS, ROWS)
        ids = [
            column(slots_ref[feature : feature + 1, where], ROWS)
            for feature in range(slots_ref.shape[0])
        ]
        for part in range(len(partners) * asked // HEAD):
            here = jnp.broadcast_to(piece_ids(starts, asked, part), (ROWS, HEAD)).astype(I16)
            hot[:, part * HEAD : (part + 1) * HEAD] = hit_counts(ids, here)
        value = mm(hot[...], rows_ref[...])
        if not first:
            value = value + sums_in[where, :]
        sums_out[where, :] = value
        if last:
            normed_ref[where, :] = normalize(value)[0].astype(BF16)
        return carry

    lax.fori_loop(0, sums_out.shape[0] // ROWS, step, 0)


def normalize(inputs):
    centred = inputs - jnp.mean(inputs, axis=-1, keepdims=True)
    inverse = lax.rsqrt(jnp.mean(centred * centred, axis=-1, keepdims=True) + epsilon)
    return (centred * inverse, inverse)


def silu_parts(inputs):
    half = inputs * 0.5
    above = 1.0 + jnp.tanh(half)
    value = half * above
    return value, above


def slope_of(inputs):
    value, above = silu_parts(inputs)
    return 0.5 * above * (1.0 + inputs - value)


def weight(w_ref, kind, mine, width):
    return w_ref[:, pl.ds(pl.multiple_of((2 * kind + mine) * width, width), width)]


def forward_body(
    place_ref, xm_ref, xo_ref, gm_ref, go_ref, w_ref, wout_ref,
    x_ref, g_ref, act_ref, att_ref, stats_ref,
):
    mine, length = place_ref[0], place_ref[1]
    count = xm_ref.shape[0]
    total = x_ref.shape[0]
    width = att_ref.shape[1]
    x_ref[rows_at(mine * count, count), :] = xm_ref[...]
    x_ref[rows_at((1 - mine) * count, count), :] = xo_ref[...]
    g_ref[rows_at(mine * count, count), :] = gm_ref[...]
    g_ref[rows_at((1 - mine) * count, count), :] = go_ref[...]

    def project(at, carry):
        where = rows_at(at * ROWS, ROWS)
        for kind in range(4):
            value, _ = silu_parts(mm(x_ref[where, :], weight(w_ref, kind, mine, width)))
            act_ref[where, kind * width : (kind + 1) * width] = value.astype(BF16)
        below = at * ROWS + lax.broadcasted_iota(jnp.int32, (ROWS, g_ref.shape[1]), 0) < length
        g_ref[where, :] = jnp.where(below, g_ref[where, :].astype(F32), 0.0).astype(BF16)
        return carry

    lax.fori_loop(0, total // ROWS, project, 0)
    half_scale = 0.5 * HEAD ** (-0.5)

    def weigh(query, keys):
        half = mm_rt(query, keys) * half_scale
        return half * (1.0 + jnp.tanh(half))

    def attend(at, carry):
        def head_cols(kind, head):
            return pl.ds(kind * width + head * HEAD, HEAD)

        heads = range(width // HEAD)
        where = rows_at(at * BLOCK, BLOCK)
        queries = [act_ref[where, head_cols(2, head)] for head in heads]

        def visit(key_at, sums):
            keys_here = rows_at(key_at * BLOCK, BLOCK)
            new = []
            for head in heads:
                weights = weigh(queries[head], act_ref[keys_here, head_cols(3, head)]).astype(BF16)
                new.append(sums[head] + mm(weights, act_ref[keys_here, head_cols(1, head)]))
            return tuple(new)

        sums = lax.fori_loop(
            0, at, visit, tuple(jnp.zeros((BLOCK, HEAD), F32) for _ in heads)
        )
        for head in heads:
            for part in range(BLOCK // ROWS):
                seen = (part + 1) * ROWS
                query = queries[head][part * ROWS : seen]
                keys_here = pl.ds(pl.multiple_of(at * BLOCK, BLOCK), seen)
                weights = weigh(query, act_ref[keys_here, head_cols(3, head)])
                ok = lax.broadcasted_iota(jnp.int32, (ROWS, seen), 1) <= (
                    part * ROWS + lax.broadcasted_iota(jnp.int32, (ROWS, seen), 0)
                )
                weights = jnp.where(ok, weights, 0.0).astype(BF16)
                att_ref[rows_at(at * BLOCK + part * ROWS, ROWS), head_cols(0, head)] = sums[head][
                    part * ROWS : seen
                ] + mm(weights, act_ref[keys_here, head_cols(1, head)])
        return carry

    lax.fori_loop(0, total // BLOCK, attend, 0)

    def measure(at, carry):
        where = rows_at(at * ROWS, ROWS)
        attended = att_ref[where, :]
        gated_grad = mm_rt(g_ref[where, :], wout_ref[rows_at(mine * width, width), :])
        t_rows = gated_grad * act_ref[where, 0:width].astype(F32)
        lane = lax.broadcasted_iota(jnp.int32, (ROWS, HEAD), 1)
        sums = jnp.zeros((ROWS, HEAD), F32)
        for at_lane, one in enumerate(
            (attended, attended * attended, t_rows, t_rows * attended)
        ):
            sums = jnp.where(lane == at_lane, jnp.sum(one, axis=1, keepdims=True), sums)
        stats_ref[:, where] = jnp.transpose(sums)[0:8, :]
        return carry

    lax.fori_loop(0, total // ROWS, measure, 0)


def backward_body(
    place_ref, x_ref, g_ref, act_ref, att_ref, stats_m_ref, stats_o_ref, w_ref, wout_ref,
    mixed_m_ref, mixed_o_ref, gx_m_ref, gx_o_ref,
    datt_ref, dgate_ref, dq_ref, dk_ref, dv_ref,
):
    mine, length = place_ref[0], place_ref[1]
    count = mixed_m_ref.shape[0]
    total, width = att_ref.shape
    hidden = 2 * width

    def middle(at, out_at, mixed_ref):
        where = rows_at(at * ROWS, ROWS)
        stats = stats_m_ref[:, where] + stats_o_ref[:, where]
        stats = jnp.transpose(
            jnp.concatenate([stats, jnp.zeros((HEAD - 8, ROWS), F32)], axis=0)
        ) * (1.0 / hidden)
        mean = stats[:, 0:1]
        inverse = lax.rsqrt(stats[:, 1:2] - mean * mean + epsilon)
        t_mean = stats[:, 2:3]
        tn_mean = inverse * (stats[:, 3:4] - mean * t_mean)
        normed = (att_ref[where, :] - mean) * inverse
        gating = act_ref[where, 0:width].astype(F32)
        gated = (normed * gating).astype(BF16)
        mixed_ref[rows_at(out_at * ROWS, ROWS), :] = mm(gated, wout_ref[rows_at(mine * width, width), :]).astype(
            mixed_ref.dtype
        )
        gated_grad = mm_rt(g_ref[where, :], wout_ref[rows_at(mine * width, width), :])
        t_rows = gated_grad * gating
        below = at * ROWS + lax.broadcasted_iota(jnp.int32, (ROWS, width), 0) < length
        datt = jnp.where(below, (t_rows - t_mean - normed * tn_mean) * inverse, 0.0)
        datt_ref[where, :] = datt.astype(BF16)
        pre = mm(x_ref[where, :], weight(w_ref, 0, mine, width))
        dgate = jnp.where(below, gated_grad * normed * slope_of(pre), 0.0)
        dgate_ref[where, :] = dgate.astype(BF16)

    def middles(at, carry):
        middle((1 - mine) * (count // ROWS) + at, at, mixed_o_ref)
        middle(mine * (count // ROWS) + at, at, mixed_m_ref)
        return carry

    lax.fori_loop(0, count // ROWS, middles, 0)
    scale = HEAD ** (-0.5)
    dq_ref[...] = jnp.zeros_like(dq_ref)

    def head_cols(kind, head):
        return pl.ds(kind * width + head * HEAD, HEAD)

    def pair(query, grad, keys, values, ok):
        scaled = mm_rt(keys, query) * scale
        value, above = silu_parts(scaled)
        weights_grad = mm_rt(values, grad)
        score_grad = weights_grad * above * (1.0 + scaled - value)
        if ok is not None:
            value = jnp.where(ok, value, 0.0)
            score_grad = jnp.where(ok, score_grad, 0.0)
        score_grad = score_grad.astype(BF16)
        return (
            mm(value.astype(BF16), grad),
            mm(score_grad, query),
            mm_lt(score_grad, keys),
        )

    def back(key_at, carry):
        heads = range(width // HEAD)
        keys_here = rows_at(key_at * BLOCK, BLOCK)
        keys = [act_ref[keys_here, head_cols(3, head)] for head in heads]
        values = [act_ref[keys_here, head_cols(1, head)] for head in heads]
        ok = lax.broadcasted_iota(jnp.int32, (BLOCK, BLOCK), 0) <= (
            lax.broadcasted_iota(jnp.int32, (BLOCK, BLOCK), 1)
        )

        def visit(at, sums, ok=None):
            where = rows_at(at * BLOCK, BLOCK)
            new = []
            for head in heads:
                more_v, more_k, more_q = pair(
                    act_ref[where, head_cols(2, head)],
                    datt_ref[where, head_cols(0, head)],
                    keys[head],
                    values[head],
                    ok,
                )
                dq_ref[where, head_cols(0, head)] += more_q
                new += [sums[2 * head] + more_v, sums[2 * head + 1] + more_k]
            return tuple(new)

        zero = tuple(jnp.zeros((BLOCK, HEAD), F32) for _ in range(2 * len(heads)))
        sums = visit(key_at, zero, ok)
        sums = lax.fori_loop(key_at + 1, total // BLOCK, visit, sums)
        for head in heads:
            dv_ref[keys_here, head_cols(0, head)] = sums[2 * head]
            dk_ref[keys_here, head_cols(0, head)] = sums[2 * head + 1]
        return carry

    lax.fori_loop(0, total // BLOCK, back, 0)

    def finish(at, out_at, gx_ref):
        where = rows_at(at * ROWS, ROWS)
        total_x = mm_rt(dgate_ref[where, :], weight(w_ref, 0, mine, width))
        for kind, grad_ref, factor in (
            (1, dv_ref, 1.0), (2, dq_ref, 0.5 * scale), (3, dk_ref, 0.5 * scale)
        ):
            columns = weight(w_ref, kind, mine, width)
            slope = slope_of(mm(x_ref[where, :], columns))
            grad = (grad_ref[where, :] * (factor * slope)).astype(BF16)
            total_x = total_x + mm_rt(grad, columns)
        gx_ref[rows_at(out_at * ROWS, ROWS), :] = total_x.astype(gx_ref.dtype)

    def finishes(at, carry):
        finish((1 - mine) * (count // ROWS) + at, at, gx_o_ref)
        finish(mine * (count // ROWS) + at, at, gx_m_ref)
        return carry

    lax.fori_loop(0, count // ROWS, finishes, 0)


def embed_back(place_ref, embedded_ref, g_ref, gx_m_ref, gx_o_ref, grads):
    count = embedded_ref.shape[0]
    first = place_ref[0] * count

    def step(at, carry):
        where = rows_at(at * ROWS, ROWS)
        normed, inverse = normalize(embedded_ref[where, :])
        grad_x = gx_m_ref[where, :].astype(F32) + gx_o_ref[where, :].astype(F32)
        back = (
            grad_x
            - jnp.mean(grad_x, axis=-1, keepdims=True)
            - normed * jnp.mean(grad_x * normed, axis=-1, keepdims=True)
        ) * inverse
        below = (
            first + at * ROWS + lax.broadcasted_iota(jnp.int32, back.shape, 0) < place_ref[1]
        )
        grads[where, :] = jnp.where(below, g_ref[where, :].astype(F32) + back, 0.0).astype(BF16)
        return carry

    lax.fori_loop(0, count // ROWS, step, 0)


def scatter_body(partners, first, asked, place_ref, slots_ref, *refs):
    refs = list(refs)
    if first:
        parts = [refs.pop(0) for _ in range(4)]
    else:
        grads = refs.pop(0)
    outs = [refs.pop(0) for _ in partners]
    if first:
        grads = refs.pop(0)
        embed_back(place_ref, *parts, grads)
    hot = refs.pop(0)
    count = grads.shape[0]
    places = lax.broadcasted_iota(jnp.int32, (asked, HEAD), 0)
    heres = [(places + (place_ref[2] ^ partner) * asked).astype(I16) for partner in partners]
    for part in range(count // HEAD):
        cols = slice(part * HEAD, (part + 1) * HEAD)
        ids = [
            jnp.broadcast_to(slots_ref[feature : feature + 1, cols], (asked, HEAD)).astype(I16)
            for feature in range(slots_ref.shape[0])
        ]
        for at, here in enumerate(heres):
            hot[at * asked : (at + 1) * asked, cols] = hit_counts(ids, here)
    rows = mm(hot[...], grads[...]).astype(BF16)
    for at, out_ref in enumerate(outs):
        out_ref[...] = rows[at * asked : (at + 1) * asked, :]


def owner_body(partners, first, last, place_ref, ids_ref, *refs):
    refs = list(refs)
    chunks = [refs.pop(0) for _ in partners]
    sums_in = None if first else refs.pop(0)
    if last:
        mine_ref, other_ref = refs.pop(0), refs.pop(0)
        table_rows = 2 * mine_ref.shape[0]
    else:
        sums_out = refs.pop(0)
        table_rows = sums_out.shape[0]
    rows_ref, hot = refs
    asked = ids_ref.shape[1]
    for at, chunk in enumerate(chunks):
        rows_ref[at * asked : (at + 1) * asked, :] = chunk[...]
    ids = jnp.concatenate(
        [ids_ref[pl.ds(place_ref[2] ^ partner, 1), :] for partner in partners], axis=1
    )
    places = lax.broadcasted_iota(jnp.int32, (ROWS, HEAD), 0)

    def rows_of(at):
        here = (places + at * ROWS).astype(I16)
        for part in range(len(partners) * asked // HEAD):
            cols = slice(part * HEAD, (part + 1) * HEAD)
            hot[:, cols] = hits(jnp.broadcast_to(ids[:, cols], (ROWS, HEAD)).astype(I16), here)
        value = mm(hot[...], rows_ref[...])
        if not first:
            value = value + sums_in[rows_at(at * ROWS, ROWS), :]
        return value

    half = table_rows // 2 // ROWS

    def step(at, carry):
        if last:
            other_ref[rows_at(at * ROWS, ROWS), :] = rows_of(
                (1 - place_ref[0]) * half + at
            ).astype(BF16)
            mine_ref[rows_at(at * ROWS, ROWS), :] = rows_of(place_ref[0] * half + at)
        else:
            for offset in range(2):
                now = 2 * at + offset
                sums_out[rows_at(now * ROWS, ROWS), :] = rows_of(now)
        return carry

    lax.fori_loop(0, half, step, 0)


def split(items, shares):
    total, groups, begin = sum(shares), [], 0
    for at in range(len(shares)):
        end = len(items) * sum(shares[: at + 1]) // total
        groups.append(items[begin:end])
        begin = end
    return groups


def swap(array):
    return lax.ppermute(array, "ctx", [(0, 1), (1, 0)])


def on_device(item_table, serve_rows, token_slots, lengths, w_proj, w_out, grad_out):
    table_rows, row_width = item_table.shape
    requesters, asked = serve_rows.shape
    row_count, features = token_slots.shape[1:]
    hidden_full = w_out.shape[0]
    assert lax.axis_size("ctx") == 2 and requesters & (requesters - 1) == 0
    assert max(table_rows, requesters * asked) < 2**15
    total = row_count * 2
    width = hidden_full // 2
    mine = lax.axis_index("ctx")
    me = lax.axis_index("table")
    place = jnp.stack([mine, lengths[0], me])
    shape = jax.ShapeDtypeStruct
    chunk = shape((asked, row_width), BF16)
    far_first = list(range(requesters - 1, 0, -1))

    def cross(array, partner):
        return lax.ppermute(
            array, "table", [(one, one ^ partner) for one in range(requesters)]
        )

    cotangent = grad_out[0]
    cotangent_o = swap(cotangent)
    slots = token_slots[0].T
    fetched = {}
    table_low = item_table
    for at, group in enumerate(split(far_first + [0], SENDS)):
        outs = [chunk] * len(group)
        if at == 0:
            outs.append(shape((table_rows, row_width), BF16))
        served = call(
            functools.partial(serve_body, tuple(group), at == 0),
            tuple(outs),
            [smem()] + [vmem()] * 2,
            [pltpu.VMEM((len(group) * asked, table_rows), BF16)],
            flops=2 * len(group) * asked * table_rows * row_width,
            moved=2 * table_rows * row_width,
        )(place, serve_rows, table_low)
        if at == 0:
            table_low = served[-1]
        for partner, rows in zip(group, served):
            fetched[partner] = cross(rows, partner) if partner else rows

    sums = None
    groups = split([0] + far_first, RECEIVES)
    for at, group in enumerate(groups):
        first, last = at == 0, at == len(groups) - 1
        outs = [shape((row_count, row_width), F32)]
        if last:
            outs.append(shape((row_count, row_width), BF16))
        made = call(
            functools.partial(embed_body, tuple(group), first, last, asked),
            tuple(outs),
            [smem()] + [vmem()] * (1 + len(group) + (not first)),
            [
                pltpu.VMEM((len(group) * asked, row_width), BF16),
                pltpu.VMEM((ROWS, len(group) * asked), BF16),
            ],
            flops=2 * len(group) * asked * row_count * row_width,
            moved=8 * row_count * row_width,
        )(place, slots, *[fetched[one] for one in group], *([] if first else [sums]))
        sums = made[0]
    embedded, normed = made

    normed_o = swap(normed)
    x_all, g_all, act, attended, stats = call(
        forward_body,
        (
            shape((total, row_width), BF16),
            shape((total, row_width), BF16),
            shape((total, 4 * width), BF16),
            shape((total, width), F32),
            shape((8, total), F32),
        ),
        [smem()] + [vmem()] * 6,
        flops=2 * total * total * width + 8 * total * row_width * width,
        moved=12 * total * width,
    )(place, normed, normed_o, cotangent, cotangent_o, w_proj, w_out)
    stats_o = swap(stats)
    part = shape((row_count, row_width), BF16)
    mixed_m, mixed_o, gx_m, gx_o = call(
        backward_body,
        (shape((row_count, row_width), F32), part, shape((row_count, row_width), F32), part),
        [smem()] + [vmem()] * 8,
        [
            pltpu.VMEM((total, width), BF16),
            pltpu.VMEM((total, width), BF16),
            pltpu.VMEM((total, width), F32),
            pltpu.VMEM((total, width), F32),
            pltpu.VMEM((total, width), F32),
        ],
        flops=5 * total * total * width + 16 * total * row_width * width,
        moved=12 * total * width,
    )(place, x_all, g_all, act, attended, stats, stats_o, w_proj, w_out)
    gx_in = swap(gx_o)
    mixed_in = swap(mixed_o)

    returned = {}
    grads = None
    for at, group in enumerate(split(far_first + [0], SENDS)):
        outs = [chunk] * len(group)
        operands = [grads]
        if at == 0:
            outs.append(shape((row_count, row_width), BF16))
            operands = [embedded, cotangent, gx_m, gx_in]
        made = call(
            functools.partial(scatter_body, tuple(group), at == 0, asked),
            tuple(outs),
            [smem()] + [vmem()] * (1 + len(operands)),
            [pltpu.VMEM((len(group) * asked, row_count), BF16)],
            flops=2 * len(group) * asked * row_count * row_width,
            moved=2 * len(group) * asked * row_width,
        )(place, slots, *operands)
        if at == 0:
            grads = made[-1]
        for partner, rows in zip(group, made):
            returned[partner] = cross(rows, partner) if partner else rows

    half_rows = table_rows // 2
    for at, group in enumerate(groups):
        first, last = at == 0, at == len(groups) - 1
        if last:
            outs = (shape((half_rows, row_width), F32), shape((half_rows, row_width), BF16))
        else:
            outs = (shape((table_rows, row_width), F32),)
        made = call(
            functools.partial(owner_body, tuple(group), first, last),
            outs,
            [smem()] + [vmem()] * (1 + len(group) + (not first)),
            [
                pltpu.VMEM((len(group) * asked, row_width), BF16),
                pltpu.VMEM((ROWS, len(group) * asked), BF16),
            ],
            flops=2 * len(group) * asked * table_rows * row_width,
            moved=8 * table_rows * row_width,
        )(place, serve_rows, *[returned[one] for one in group], *([] if first else [sums]))
        sums = made[0]
    owner_m, owner_o = made
    grad_table = owner_m + swap(owner_o).astype(F32)
    positions = mine * row_count + jnp.arange(row_count, dtype=jnp.int32)
    layer_out = jnp.where(
        (positions < lengths[0])[:, None], embedded + (mixed_m + mixed_in.astype(F32)), 0.0
    ).astype(BF16)
    return (layer_out[None], grad_table)


def solution(mesh):
    placed = (
        P("table", None),
        P("table", "ctx"),
        P("table", "ctx", None),
        P("table"),
        P(),
        P(),
        P("table", "ctx", None),
    )
    return jax.shard_map(
        on_device,
        mesh=mesh,
        in_specs=placed,
        out_specs=(P("table", "ctx", None), P(("table", "ctx"), None)),
        check_vma=False,
    )
```

```python
import functools

import jax
import jax.numpy as jnp
from jax import lax
from jax.experimental import pallas as pl
from jax.experimental.pallas import tpu as pltpu
from jax.sharding import PartitionSpec as P

HEAD = 128
epsilon = 1e-05
F32 = jnp.float32
BF16 = jnp.bfloat16
I16 = jnp.int16
ROWS = 256
BLOCK = 512
SENDS = (1, 3, 5, 7)


def mm(lhs, rhs):
    return lax.dot_general(lhs, rhs, (((1,), (0,)), ((), ())), preferred_element_type=F32)


def mm_rt(lhs, rhs):
    return lax.dot_general(lhs, rhs, (((1,), (1,)), ((), ())), preferred_element_type=F32)


def mm_lt(lhs, rhs):
    return lax.dot_general(lhs, rhs, (((0,), (0,)), ((), ())), preferred_element_type=F32)


def rows_at(start, count):
    return pl.ds(pl.multiple_of(start, count), count)


def vmem():
    return pl.BlockSpec(memory_space=pltpu.VMEM)


def smem():
    return pl.BlockSpec(memory_space=pltpu.SMEM)


def call(body, out_shape, in_specs, scratch=(), flops=0, moved=0):
    return pl.pallas_call(
        body,
        out_shape=out_shape,
        in_specs=in_specs,
        out_specs=jax.tree.map(lambda _: vmem(), out_shape),
        scratch_shapes=list(scratch),
        compiler_params=pltpu.CompilerParams(vmem_limit_bytes=60 * 1024 * 1024),
        cost_estimate=pl.CostEstimate(flops=flops, bytes_accessed=moved, transcendentals=0),
    )


def column(row, count):
    return jnp.transpose(jnp.broadcast_to(row, (HEAD, count))).astype(I16)


def hits(ids, here):
    return jnp.where(ids == here, jnp.ones((), BF16), jnp.zeros((), BF16))


def hit_counts(all_ids, here):
    found = [hits(ids, here) for ids in all_ids]
    while len(found) > 1:
        found = [sum(found[at : at + 2][1:], found[at]) for at in range(0, len(found), 2)]
    return found[0]


def piece_ids(piece_starts, asked, part):
    lane = lax.broadcasted_iota(jnp.int32, (1, HEAD), 1)
    first = part * HEAD // asked
    here = lane + (piece_starts[first] + part * HEAD - first * asked)
    for piece in range(first + 1, -(-(part + 1) * HEAD // asked)):
        begin = piece * asked - part * HEAD
        here = jnp.where(lane >= begin, lane + (piece_starts[piece] - begin), here)
    return here


def serve_body(partners, cast, place_ref, ids_ref, table_ref, *refs):
    outs, hot = refs[: len(partners)], refs[-1]
    if cast:
        low_ref = refs[len(partners)]
        low_ref[...] = table_ref[...].astype(BF16)
    else:
        low_ref = table_ref
    asked = ids_ref.shape[1]
    lanes = lax.broadcasted_iota(jnp.int32, (asked, HEAD), 1).astype(I16)
    for at, partner in enumerate(partners):
        ids = column(ids_ref[pl.ds(place_ref[2] ^ partner, 1), :], asked)
        for part in range(table_ref.shape[0] // HEAD):
            hot[at * asked : (at + 1) * asked, part * HEAD : (part + 1) * HEAD] = hits(
                ids, lanes + jnp.int16(part * HEAD)
            )
    rows = mm(hot[...], low_ref[...]).astype(BF16)
    for at, out_ref in enumerate(outs):
        out_ref[...] = rows[at * asked : (at + 1) * asked, :]


def embed_body(partners, first, last, asked, place_ref, slots_ref, *refs):
    refs = list(refs)
    chunks = [refs.pop(0) for _ in partners]
    sums_in = None if first else refs.pop(0)
    sums_out = refs.pop(0)
    normed_ref = refs.pop(0) if last else None
    rows_ref, hot = refs
    starts = [(place_ref[2] ^ partner) * asked for partner in partners]
    for at, chunk in enumerate(chunks):
        rows_ref[at * asked : (at + 1) * asked, :] = chunk[...]

    def step(at, carry):
        where = rows_at(at * ROWS, ROWS)
        ids = [
            column(slots_ref[feature : feature + 1, where], ROWS)
            for feature in range(slots_ref.shape[0])
        ]
        for part in range(len(partners) * asked // HEAD):
            here = jnp.broadcast_to(piece_ids(starts, asked, part), (ROWS, HEAD)).astype(I16)
            hot[:, part * HEAD : (part + 1) * HEAD] = hit_counts(ids, here)
        value = mm(hot[...], rows_ref[...])
        if not first:
            value = value + sums_in[where, :]
        sums_out[where, :] = value
        if last:
            normed_ref[where, :] = normalize(value)[0].astype(BF16)
        return carry

    lax.fori_loop(0, sums_out.shape[0] // ROWS, step, 0)


def normalize(inputs):
    centred = inputs - jnp.mean(inputs, axis=-1, keepdims=True)
    inverse = lax.rsqrt(jnp.mean(centred * centred, axis=-1, keepdims=True) + epsilon)
    return (centred * inverse, inverse)


def silu_parts(inputs):
    half = inputs * 0.5
    above = 1.0 + jnp.tanh(half)
    value = half * above
    return value, above


def slope_of(inputs):
    value, above = silu_parts(inputs)
    return 0.5 * above * (1.0 + inputs - value)


def weight(w_ref, kind, mine, width):
    return w_ref[:, pl.ds(pl.multiple_of((2 * kind + mine) * width, width), width)]


def forward_body(
    place_ref, xm_ref, xo_ref, gm_ref, go_ref, w_ref, wout_ref,
    x_ref, g_ref, act_ref, att_ref, stats_ref,
):
    mine, length = place_ref[0], place_ref[1]
    count = xm_ref.shape[0]
    total = x_ref.shape[0]
    width = att_ref.shape[1]
    x_ref[rows_at(mine * count, count), :] = xm_ref[...]
    x_ref[rows_at((1 - mine) * count, count), :] = xo_ref[...]
    g_ref[rows_at(mine * count, count), :] = gm_ref[...]
    g_ref[rows_at((1 - mine) * count, count), :] = go_ref[...]

    def project(at, carry):
        where = rows_at(at * ROWS, ROWS)
        for kind in range(4):
            value, _ = silu_parts(mm(x_ref[where, :], weight(w_ref, kind, mine, width)))
            act_ref[where, kind * width : (kind + 1) * width] = value.astype(BF16)
        below = at * ROWS + lax.broadcasted_iota(jnp.int32, (ROWS, g_ref.shape[1]), 0) < length
        g_ref[where, :] = jnp.where(below, g_ref[where, :].astype(F32), 0.0).astype(BF16)
        return carry

    lax.fori_loop(0, total // ROWS, project, 0)
    half_scale = 0.5 * HEAD ** (-0.5)

    def weigh(query, keys):
        half = mm_rt(query, keys) * half_scale
        return half * (1.0 + jnp.tanh(half))

    def attend(at, carry):
        def head_cols(kind, head):
            return pl.ds(kind * width + head * HEAD, HEAD)

        heads = range(width // HEAD)
        where = rows_at(at * BLOCK, BLOCK)
        queries = [act_ref[where, head_cols(2, head)] for head in heads]

        def visit(key_at, sums):
            keys_here = rows_at(key_at * BLOCK, BLOCK)
            new = []
            for head in heads:
                weights = weigh(queries[head], act_ref[keys_here, head_cols(3, head)]).astype(BF16)
                new.append(sums[head] + mm(weights, act_ref[keys_here, head_cols(1, head)]))
            return tuple(new)

        sums = lax.fori_loop(
            0, at, visit, tuple(jnp.zeros((BLOCK, HEAD), F32) for _ in heads)
        )
        for head in heads:
            for part in range(BLOCK // ROWS):
                seen = (part + 1) * ROWS
                query = queries[head][part * ROWS : seen]
                keys_here = pl.ds(pl.multiple_of(at * BLOCK, BLOCK), seen)
                weights = weigh(query, act_ref[keys_here, head_cols(3, head)])
                ok = lax.broadcasted_iota(jnp.int32, (ROWS, seen), 1) <= (
                    part * ROWS + lax.broadcasted_iota(jnp.int32, (ROWS, seen), 0)
                )
                weights = jnp.where(ok, weights, 0.0).astype(BF16)
                att_ref[rows_at(at * BLOCK + part * ROWS, ROWS), head_cols(0, head)] = sums[head][
                    part * ROWS : seen
                ] + mm(weights, act_ref[keys_here, head_cols(1, head)])
        return carry

    lax.fori_loop(0, total // BLOCK, attend, 0)

    def measure(at, carry):
        where = rows_at(at * ROWS, ROWS)
        attended = att_ref[where, :]
        gated_grad = mm_rt(g_ref[where, :], wout_ref[rows_at(mine * width, width), :])
        t_rows = gated_grad * act_ref[where, 0:width].astype(F32)
        lane = lax.broadcasted_iota(jnp.int32, (ROWS, HEAD), 1)
        sums = jnp.zeros((ROWS, HEAD), F32)
        for at_lane, one in enumerate(
            (attended, attended * attended, t_rows, t_rows * attended)
        ):
            sums = jnp.where(lane == at_lane, jnp.sum(one, axis=1, keepdims=True), sums)
        stats_ref[:, where] = jnp.transpose(sums)[0:8, :]
        return carry

    lax.fori_loop(0, total // ROWS, measure, 0)


def backward_body(
    place_ref, x_ref, g_ref, act_ref, att_ref, stats_m_ref, stats_o_ref, w_ref, wout_ref,
    mixed_m_ref, mixed_o_ref, gx_m_ref, gx_o_ref,
    datt_ref, dgate_ref, dq_ref, dk_ref, dv_ref,
):
    mine, length = place_ref[0], place_ref[1]
    count = mixed_m_ref.shape[0]
    total, width = att_ref.shape
    hidden = 2 * width

    def middle(at, out_at, mixed_ref):
        where = rows_at(at * ROWS, ROWS)
        stats = stats_m_ref[:, where] + stats_o_ref[:, where]
        stats = jnp.transpose(
            jnp.concatenate([stats, jnp.zeros((HEAD - 8, ROWS), F32)], axis=0)
        ) * (1.0 / hidden)
        mean = stats[:, 0:1]
        inverse = lax.rsqrt(stats[:, 1:2] - mean * mean + epsilon)
        t_mean = stats[:, 2:3]
        tn_mean = inverse * (stats[:, 3:4] - mean * t_mean)
        normed = (att_ref[where, :] - mean) * inverse
        gating = act_ref[where, 0:width].astype(F32)
        gated = (normed * gating).astype(BF16)
        mixed_ref[rows_at(out_at * ROWS, ROWS), :] = mm(gated, wout_ref[rows_at(mine * width, width), :]).astype(
            mixed_ref.dtype
        )
        gated_grad = mm_rt(g_ref[where, :], wout_ref[rows_at(mine * width, width), :])
        t_rows = gated_grad * gating
        below = at * ROWS + lax.broadcasted_iota(jnp.int32, (ROWS, width), 0) < length
        datt = jnp.where(below, (t_rows - t_mean - normed * tn_mean) * inverse, 0.0)
        datt_ref[where, :] = datt.astype(BF16)
        pre = mm(x_ref[where, :], weight(w_ref, 0, mine, width))
        dgate = jnp.where(below, gated_grad * normed * slope_of(pre), 0.0)
        dgate_ref[where, :] = dgate.astype(BF16)

    def middles(at, carry):
        middle((1 - mine) * (count // ROWS) + at, at, mixed_o_ref)
        middle(mine * (count // ROWS) + at, at, mixed_m_ref)
        return carry

    lax.fori_loop(0, count // ROWS, middles, 0)
    scale = HEAD ** (-0.5)
    dq_ref[...] = jnp.zeros_like(dq_ref)

    def head_cols(kind, head):
        return pl.ds(kind * width + head * HEAD, HEAD)

    def pair(query, grad, keys, values, ok):
        scaled = mm_rt(keys, query) * scale
        value, above = silu_parts(scaled)
        weights_grad = mm_rt(values, grad)
        score_grad = weights_grad * above * (1.0 + scaled - value)
        if ok is not None:
            value = jnp.where(ok, value, 0.0)
            score_grad = jnp.where(ok, score_grad, 0.0)
        score_grad = score_grad.astype(BF16)
        return (
            mm(value.astype(BF16), grad),
            mm(score_grad, query),
            mm_lt(score_grad, keys),
        )

    def back(key_at, carry):
        heads = range(width // HEAD)
        keys_here = rows_at(key_at * BLOCK, BLOCK)
        keys = [act_ref[keys_here, head_cols(3, head)] for head in heads]
        values = [act_ref[keys_here, head_cols(1, head)] for head in heads]
        ok = lax.broadcasted_iota(jnp.int32, (BLOCK, BLOCK), 0) <= (
            lax.broadcasted_iota(jnp.int32, (BLOCK, BLOCK), 1)
        )

        def visit(at, sums, ok=None):
            where = rows_at(at * BLOCK, BLOCK)
            new = []
            for head in heads:
                more_v, more_k, more_q = pair(
                    act_ref[where, head_cols(2, head)],
                    datt_ref[where, head_cols(0, head)],
                    keys[head],
                    values[head],
                    ok,
                )
                dq_ref[where, head_cols(0, head)] += more_q
                new += [sums[2 * head] + more_v, sums[2 * head + 1] + more_k]
            return tuple(new)

        zero = tuple(jnp.zeros((BLOCK, HEAD), F32) for _ in range(2 * len(heads)))
        sums = visit(key_at, zero, ok)
        sums = lax.fori_loop(key_at + 1, total // BLOCK, visit, sums)
        for head in heads:
            dv_ref[keys_here, head_cols(0, head)] = sums[2 * head]
            dk_ref[keys_here, head_cols(0, head)] = sums[2 * head + 1]
        return carry

    lax.fori_loop(0, total // BLOCK, back, 0)

    def finish(at, out_at, gx_ref):
        where = rows_at(at * ROWS, ROWS)
        total_x = mm_rt(dgate_ref[where, :], weight(w_ref, 0, mine, width))
        for kind, grad_ref, factor in (
            (1, dv_ref, 1.0), (2, dq_ref, 0.5 * scale), (3, dk_ref, 0.5 * scale)
        ):
            columns = weight(w_ref, kind, mine, width)
            slope = slope_of(mm(x_ref[where, :], columns))
            grad = (grad_ref[where, :] * (factor * slope)).astype(BF16)
            total_x = total_x + mm_rt(grad, columns)
        gx_ref[rows_at(out_at * ROWS, ROWS), :] = total_x.astype(gx_ref.dtype)

    def finishes(at, carry):
        finish((1 - mine) * (count // ROWS) + at, at, gx_o_ref)
        finish(mine * (count // ROWS) + at, at, gx_m_ref)
        return carry

    lax.fori_loop(0, count // ROWS, finishes, 0)


def embed_back(place_ref, embedded_ref, g_ref, gx_m_ref, gx_o_ref, grads):
    count = embedded_ref.shape[0]
    first = place_ref[0] * count

    def step(at, carry):
        where = rows_at(at * ROWS, ROWS)
        normed, inverse = normalize(embedded_ref[where, :])
        grad_x = gx_m_ref[where, :].astype(F32) + gx_o_ref[where, :].astype(F32)
        back = (
            grad_x
            - jnp.mean(grad_x, axis=-1, keepdims=True)
            - normed * jnp.mean(grad_x * normed, axis=-1, keepdims=True)
        ) * inverse
        below = (
            first + at * ROWS + lax.broadcasted_iota(jnp.int32, back.shape, 0) < place_ref[1]
        )
        grads[where, :] = jnp.where(below, g_ref[where, :].astype(F32) + back, 0.0).astype(BF16)
        return carry

    lax.fori_loop(0, count // ROWS, step, 0)


def scatter_body(partners, first, asked, place_ref, slots_ref, *refs):
    refs = list(refs)
    if first:
        parts = [refs.pop(0) for _ in range(4)]
    else:
        grads = refs.pop(0)
    outs = [refs.pop(0) for _ in partners]
    if first:
        grads = refs.pop(0)
        embed_back(place_ref, *parts, grads)
    hot = refs.pop(0)
    count = grads.shape[0]
    places = lax.broadcasted_iota(jnp.int32, (asked, HEAD), 0)
    heres = [(places + (place_ref[2] ^ partner) * asked).astype(I16) for partner in partners]
    for part in range(count // HEAD):
        cols = slice(part * HEAD, (part + 1) * HEAD)
        ids = [
            jnp.broadcast_to(slots_ref[feature : feature + 1, cols], (asked, HEAD)).astype(I16)
            for feature in range(slots_ref.shape[0])
        ]
        for at, here in enumerate(heres):
            hot[at * asked : (at + 1) * asked, cols] = hit_counts(ids, here)
    rows = mm(hot[...], grads[...]).astype(BF16)
    for at, out_ref in enumerate(outs):
        out_ref[...] = rows[at * asked : (at + 1) * asked, :]


def owner_body(partners, first, last, place_ref, ids_ref, *refs):
    refs = list(refs)
    chunks = [refs.pop(0) for _ in partners]
    sums_in = None if first else refs.pop(0)
    if last:
        mine_ref, other_ref = refs.pop(0), refs.pop(0)
        table_rows = 2 * mine_ref.shape[0]
    else:
        sums_out = refs.pop(0)
        table_rows = sums_out.shape[0]
    rows_ref, hot = refs
    asked = ids_ref.shape[1]
    for at, chunk in enumerate(chunks):
        rows_ref[at * asked : (at + 1) * asked, :] = chunk[...]
    ids = jnp.concatenate(
        [ids_ref[pl.ds(place_ref[2] ^ partner, 1), :] for partner in partners], axis=1
    )
    places = lax.broadcasted_iota(jnp.int32, (ROWS, HEAD), 0)

    def rows_of(at):
        here = (places + at * ROWS).astype(I16)
        for part in range(len(partners) * asked // HEAD):
            cols = slice(part * HEAD, (part + 1) * HEAD)
            hot[:, cols] = hits(jnp.broadcast_to(ids[:, cols], (ROWS, HEAD)).astype(I16), here)
        value = mm(hot[...], rows_ref[...])
        if not first:
            value = value + sums_in[rows_at(at * ROWS, ROWS), :]
        return value

    half = table_rows // 2 // ROWS

    def step(at, carry):
        if last:
            other_ref[rows_at(at * ROWS, ROWS), :] = rows_of(
                (1 - place_ref[0]) * half + at
            ).astype(BF16)
            mine_ref[rows_at(at * ROWS, ROWS), :] = rows_of(place_ref[0] * half + at)
        else:
            for offset in range(2):
                now = 2 * at + offset
                sums_out[rows_at(now * ROWS, ROWS), :] = rows_of(now)
        return carry

    lax.fori_loop(0, half, step, 0)


def split(items, shares):
    total, groups, begin = sum(shares), [], 0
    for at in range(len(shares)):
        end = len(items) * sum(shares[: at + 1]) // total
        groups.append(items[begin:end])
        begin = end
    return groups


def swap(array):
    return lax.ppermute(array, "ctx", [(0, 1), (1, 0)])


def on_device(item_table, serve_rows, token_slots, lengths, w_proj, w_out, grad_out):
    table_rows, row_width = item_table.shape
    requesters, asked = serve_rows.shape
    row_count, features = token_slots.shape[1:]
    hidden_full = w_out.shape[0]
    assert lax.axis_size("ctx") == 2 and requesters & (requesters - 1) == 0
    assert max(table_rows, requesters * asked) < 2**15
    total = row_count * 2
    width = hidden_full // 2
    mine = lax.axis_index("ctx")
    me = lax.axis_index("table")
    place = jnp.stack([mine, lengths[0], me])
    shape = jax.ShapeDtypeStruct
    chunk = shape((asked, row_width), BF16)
    far_first = list(range(requesters - 1, 0, -1))

    def cross(array, partner):
        return lax.ppermute(
            array, "table", [(one, one ^ partner) for one in range(requesters)]
        )

    cotangent = grad_out[0]
    cotangent_o = swap(cotangent)
    slots = token_slots[0].T
    fetched = {}
    table_low = item_table
    for at, group in enumerate(split(far_first + [0], SENDS)):
        outs = [chunk] * len(group)
        if at == 0:
            outs.append(shape((table_rows, row_width), BF16))
        served = call(
            functools.partial(serve_body, tuple(group), at == 0),
            tuple(outs),
            [smem()] + [vmem()] * 2,
            [pltpu.VMEM((len(group) * asked, table_rows), BF16)],
            flops=2 * len(group) * asked * table_rows * row_width,
            moved=2 * table_rows * row_width,
        )(place, serve_rows, table_low)
        if at == 0:
            table_low = served[-1]
        for partner, rows in zip(group, served):
            fetched[partner] = cross(rows, partner) if partner else rows

    sums = None
    late = [one for one in far_first if requesters // 2 <= one < requesters * 3 // 4]
    groups = [[0] + [one for one in far_first if one not in late], late]
    for at, group in enumerate(groups):
        first, last = at == 0, at == len(groups) - 1
        outs = [shape((row_count, row_width), F32)]
        if last:
            outs.append(shape((row_count, row_width), BF16))
        made = call(
            functools.partial(embed_body, tuple(group), first, last, asked),
            tuple(outs),
            [smem()] + [vmem()] * (1 + len(group) + (not first)),
            [
                pltpu.VMEM((len(group) * asked, row_width), BF16),
                pltpu.VMEM((ROWS, len(group) * asked), BF16),
            ],
            flops=2 * len(group) * asked * row_count * row_width,
            moved=8 * row_count * row_width,
        )(place, slots, *[fetched[one] for one in group], *([] if first else [sums]))
        sums = made[0]
    embedded, normed = made

    normed_o = swap(normed)
    x_all, g_all, act, attended, stats = call(
        forward_body,
        (
            shape((total, row_width), BF16),
            shape((total, row_width), BF16),
            shape((total, 4 * width), BF16),
            shape((total, width), F32),
            shape((8, total), F32),
        ),
        [smem()] + [vmem()] * 6,
        flops=2 * total * total * width + 8 * total * row_width * width,
        moved=12 * total * width,
    )(place, normed, normed_o, cotangent, cotangent_o, w_proj, w_out)
    stats_o = swap(stats)
    part = shape((row_count, row_width), BF16)
    mixed_m, mixed_o, gx_m, gx_o = call(
        backward_body,
        (shape((row_count, row_width), F32), part, shape((row_count, row_width), F32), part),
        [smem()] + [vmem()] * 8,
        [
            pltpu.VMEM((total, width), BF16),
            pltpu.VMEM((total, width), BF16),
            pltpu.VMEM((total, width), F32),
            pltpu.VMEM((total, width), F32),
            pltpu.VMEM((total, width), F32),
        ],
        flops=5 * total * total * width + 16 * total * row_width * width,
        moved=12 * total * width,
    )(place, x_all, g_all, act, attended, stats, stats_o, w_proj, w_out)
    gx_in = swap(gx_o)
    mixed_in = swap(mixed_o)

    returned = {}
    grads = None
    for at, group in enumerate(split(far_first + [0], SENDS)):
        outs = [chunk] * len(group)
        operands = [grads]
        if at == 0:
            outs.append(shape((row_count, row_width), BF16))
            operands = [embedded, cotangent, gx_m, gx_in]
        made = call(
            functools.partial(scatter_body, tuple(group), at == 0, asked),
            tuple(outs),
            [smem()] + [vmem()] * (1 + len(operands)),
            [pltpu.VMEM((len(group) * asked, row_count), BF16)],
            flops=2 * len(group) * asked * row_count * row_width,
            moved=2 * len(group) * asked * row_width,
        )(place, slots, *operands)
        if at == 0:
            grads = made[-1]
        for partner, rows in zip(group, made):
            returned[partner] = cross(rows, partner) if partner else rows

    half_rows = table_rows // 2
    for at, group in enumerate(groups):
        first, last = at == 0, at == len(groups) - 1
        if last:
            outs = (shape((half_rows, row_width), F32), shape((half_rows, row_width), BF16))
        else:
            outs = (shape((table_rows, row_width), F32),)
        made = call(
            functools.partial(owner_body, tuple(group), first, last),
            outs,
            [smem()] + [vmem()] * (1 + len(group) + (not first)),
            [
                pltpu.VMEM((len(group) * asked, row_width), BF16),
                pltpu.VMEM((ROWS, len(group) * asked), BF16),
            ],
            flops=2 * len(group) * asked * table_rows * row_width,
            moved=8 * table_rows * row_width,
        )(place, serve_rows, *[returned[one] for one in group], *([] if first else [sums]))
        sums = made[0]
    owner_m, owner_o = made
    grad_table = owner_m + swap(owner_o).astype(F32)
    positions = mine * row_count + jnp.arange(row_count, dtype=jnp.int32)
    layer_out = jnp.where(
        (positions < lengths[0])[:, None], embedded + (mixed_m + mixed_in.astype(F32)), 0.0
    ).astype(BF16)
    return (layer_out[None], grad_table)


def solution(mesh):
    placed = (
        P("table", None),
        P("table", "ctx"),
        P("table", "ctx", None),
        P("table"),
        P(),
        P(),
        P("table", "ctx", None),
    )
    return jax.shard_map(
        on_device,
        mesh=mesh,
        in_specs=placed,
        out_specs=(P("table", "ctx", None), P(("table", "ctx"), None)),
        check_vma=False,
    )
```
